256 devices in a mesh: ctx: 32 (over z, x), head: 8 (over y, core).
Axes of the slice: x: 4, y: 4, z: 8, core: 2. Of those that a mesh axis runs over, the one named last changes fastest.
Arguments:
- tokens: bfloat16 [131072, 1024], P(('ctx', 'head')), may hold values from -16 to 16
- w_query: bfloat16 [1024, 1024], replicated, may hold values from -0.4375 to 0.4375
- w_key: bfloat16 [1024, 1024], replicated, may hold values from -0.1875 to 0.1875
- w_value: bfloat16 [1024, 1024], replicated, may hold values from -0.1875 to 0.1875
- w_out: bfloat16 [1024, 1024], replicated, may hold values from -0.1875 to 0.1875
- random_tiles: int32 [1024, 12], replicated, may hold values from 2 to 1023, as said below
- random_count: int32 [1024], replicated, may hold values from 1 to 12, as said below
Outputs:
- sublayer_out: bfloat16 [131072, 1024], P(('ctx', 'head'))
The draws below stay inside these ranges and needn't reach their ends.
Inputs may be any that keep to these rules, and one draw needn't show every extreme that they name: `random_tiles`: entry [t, j] names a tile of the sequence (tiles of ctx shard c are c * 32 to (c + 1) * 32 - 1). Entries j < random_count[t] are live: distinct within a row, never one of the first 2 tiles, and never on query tile t's own ctx shard; later entries are padding, drawn in the same way. The live entries of the 32 query tiles of one ctx shard name at most 3 distinct tiles on any one ctx shard, and in every draw some ctx shard names exactly 3 on each of the 31 other shards. `random_count`: number of live entries in each row of random_tiles; in every draw all counts of some ctx shard equal 12.
All inputs are finite; a program needn't handle non-finite values.
Results may differ from the reference program's by a relative error of at most 0.011.
Values may be sent and summed in bfloat16 or wider, within the bound.
No kernel may reach another device: no remote copies, remote signals or barrier semaphores. Data moves between devices by JAX's collectives and lax.ppermute only.
A program may use at most 128 MiB of HBM per device.

```python
import jax
import jax.numpy as jnp
from jax import lax

D = 1024
HEADS = 16
HEAD_DIM = 64
TILE = 128
GLOBALS = 2
RANDOM = 12
CAP = 3
TILES_DEV = 32
SEQ = 131072
N_CTX = 32


def pattern_pieces(key):
    base_key = jax.random.fold_in(key, 11)
    heavy_key, full_key, tail_key, order_key, count_key = jax.random.split(base_key, 5)
    heavy = jax.random.randint(heavy_key, (), 0, N_CTX)
    pair_count = (N_CTX - 1) * CAP
    full_keys = jax.random.split(full_key, N_CTX * N_CTX)
    full_sets = jax.vmap(lambda subkey: jax.random.permutation(subkey, TILES_DEV)[:CAP])(full_keys)
    full_sets = full_sets.reshape(N_CTX, N_CTX, CAP)
    tail_keys = jax.random.split(tail_key, N_CTX * N_CTX)
    tail_sets = jax.vmap(lambda subkey: jax.random.permutation(subkey, TILES_DEV - GLOBALS)[:CAP])(tail_keys)
    tail_sets = GLOBALS + tail_sets.reshape(N_CTX, N_CTX, CAP)
    source_ids = jnp.arange(N_CTX)
    chosen = jnp.where((source_ids == 0)[None, :, None], tail_sets, full_sets)
    order_keys = jax.random.split(order_key, N_CTX)
    orders = jax.vmap(lambda subkey: jax.random.permutation(subkey, pair_count))(order_keys)
    positions = (jnp.arange(TILES_DEV)[:, None] * RANDOM + jnp.arange(RANDOM)[None, :]) % pair_count
    pairs = orders[:, positions]
    stride = pairs % (N_CTX - 1)
    member = pairs // (N_CTX - 1)
    dests = jnp.arange(N_CTX)[:, None, None]
    sources = (dests + 1 + stride) % N_CTX
    local_ids = chosen[dests, sources, member]
    tiles = (sources * TILES_DEV + local_ids).reshape(N_CTX * TILES_DEV, RANDOM).astype(jnp.int32)
    counts = jax.random.randint(count_key, (N_CTX, TILES_DEV), 1, RANDOM + 1)
    counts = jnp.where(jnp.arange(N_CTX)[:, None] == heavy, RANDOM, counts)
    return (tiles, counts.reshape(-1).astype(jnp.int32))


def draw_random_tiles(key, part):
    return pattern_pieces(key)[0]


def draw_random_count(key, part):
    return pattern_pieces(key)[1]


def draw_tokens(key, part):
    drawn_key = jax.random.fold_in(jax.random.fold_in(key, 3), 0)
    drawn = jax.random.truncated_normal(drawn_key, -6.0, 6.0, (SEQ, D), jnp.float32)
    return jnp.clip(drawn, -16.0, 16.0).astype(jnp.bfloat16)


def bell_draw(key, extent, deviation, limit, held_as=jnp.bfloat16):
    return jnp.clip(deviation * jax.random.normal(key, extent, jnp.float32), -limit, limit).astype(held_as)


def setup_inputs(seed: int = 0) -> dict:
    seeds = jax.random.split(jax.random.key(seed), 8)
    return {
        "tokens": draw_tokens(jax.random.fold_in(seeds[7], 71), 0),
        "w_query": bell_draw(seeds[1], (D, D), (D // 6) ** -0.5, 0.4375),
        "w_key": bell_draw(seeds[2], (D, D), D ** -0.5, 0.1875),
        "w_value": bell_draw(seeds[3], (D, D), D ** -0.5, 0.1875),
        "w_out": bell_draw(seeds[4], (D, D), D ** -0.5, 0.1875),
        "random_tiles": draw_random_tiles(jax.random.fold_in(seeds[7], 71), 0),
        "random_count": draw_random_count(jax.random.fold_in(seeds[7], 71), 0),
    }


def reference(tokens, w_query, w_key, w_value, w_out, random_tiles, random_count):
    seq_rows = tokens.shape[0]
    tiles_total = seq_rows // TILE
    queries = jnp.dot(tokens, w_query, preferred_element_type=jnp.float32).astype(jnp.bfloat16)
    key_rows = jnp.dot(tokens, w_key, preferred_element_type=jnp.float32).astype(jnp.bfloat16)
    value_rows = jnp.dot(tokens, w_value, preferred_element_type=jnp.float32).astype(jnp.bfloat16)
    tile_ids = jnp.arange(tiles_total, dtype=jnp.int32)
    window_ids = tile_ids[:, None] + jnp.arange(-1, 2, dtype=jnp.int32)[None, :]
    window_ok = (window_ids >= GLOBALS) & (window_ids < tiles_total)
    window_ids = jnp.clip(window_ids, 0, tiles_total - 1).astype(jnp.int32)
    global_ids = jnp.broadcast_to(jnp.arange(GLOBALS, dtype=jnp.int32)[None, :], (tiles_total, GLOBALS))
    live_slots = jnp.arange(RANDOM, dtype=jnp.int32)[None, :] < random_count[:, None]
    key_ids = jnp.concatenate([window_ids, global_ids, random_tiles.astype(jnp.int32)], axis=1)
    key_ok = jnp.concatenate([window_ok, jnp.ones((tiles_total, GLOBALS), jnp.bool_), live_slots], axis=1)
    query_tiles = queries.reshape(tiles_total, TILE, HEADS, HEAD_DIM)
    key_tiles = key_rows.reshape(tiles_total, TILE, HEADS, HEAD_DIM)
    value_tiles = value_rows.reshape(tiles_total, TILE, HEADS, HEAD_DIM)
    score_scale = HEAD_DIM ** -0.5

    def one_tile(inputs):
        query_tile, tile_list, tile_ok = inputs
        gathered_keys = key_tiles[tile_list].reshape(-1, HEADS, HEAD_DIM).astype(jnp.float32)
        gathered_values = value_tiles[tile_list].reshape(-1, HEADS, HEAD_DIM).astype(jnp.float32)
        scores = jnp.einsum("qhd,khd->hqk", query_tile.astype(jnp.float32), gathered_keys) * score_scale
        row_ok = jnp.repeat(tile_ok, TILE)
        scores = jnp.where(row_ok[None, None, :], scores, -1e30)
        maxima = jnp.max(scores, axis=-1, keepdims=True)
        weights = jnp.exp(scores - maxima)
        totals = jnp.sum(weights, axis=-1)
        rounded = lax.optimization_barrier(weights.astype(jnp.bfloat16)).astype(jnp.float32)
        blended = jnp.einsum("hqk,khd->qhd", rounded, gathered_values)
        blended = blended / jnp.transpose(totals)[:, :, None]
        return blended.astype(jnp.bfloat16).reshape(TILE, HEADS * HEAD_DIM)

    attended = lax.map(one_tile, (query_tiles, key_ids, key_ok)).reshape(seq_rows, HEADS * HEAD_DIM)
    return jnp.dot(attended, w_out, preferred_element_type=jnp.float32).astype(jnp.bfloat16)
```

```python
import jax
import jax.numpy as jnp
from jax import lax
from jax.experimental import pallas as pl
from jax.experimental.pallas import tpu as pltpu
from jax.sharding import PartitionSpec as P

HEADS = 16
HEAD_DIM = 64
TILE = 128
GLOBALS = 2
RANDOM = 12
CAP = 3
LOG2E = 1.4426950408889634
SCALE = HEAD_DIM ** (-0.5) * LOG2E
NEG = -1e30


def project_kv_kernel(x_ref, wk_ref, wv_ref, o_ref):
    w = jnp.concatenate([wk_ref[...], wv_ref[...]], axis=1)
    o_ref[0] = jnp.dot(x_ref[...], w, preferred_element_type=jnp.float32).astype(jnp.bfloat16)


def project_kv(x, w_key, w_value, groups):
    rows, width = x.shape
    lanes = w_key.shape[1] // groups
    w_spec = pl.BlockSpec((width, lanes), lambda h: (0, h))
    return pl.pallas_call(
        project_kv_kernel,
        grid=(groups,),
        in_specs=[pl.BlockSpec((rows, width), lambda h: (0, 0)), w_spec, w_spec],
        out_specs=pl.BlockSpec((1, rows, 2 * lanes), lambda h: (h, 0, 0)),
        out_shape=jax.ShapeDtypeStruct((groups, rows, 2 * lanes), jnp.bfloat16),
        cost_estimate=pl.CostEstimate(
            flops=4 * rows * width * w_key.shape[1],
            transcendentals=0,
            bytes_accessed=4 * width * w_key.shape[1] + 6 * rows * width,
        ),
        name="project_kv",
    )(x, w_key, w_value)


def project_q_kernel(x_ref, wa_ref, wb_ref, o_ref):
    lanes = wa_ref.shape[1]
    w = jnp.concatenate([wa_ref[...], wb_ref[...]], axis=1)
    r = jnp.dot(x_ref[...], w, preferred_element_type=jnp.float32).astype(jnp.bfloat16)
    o_ref[0] = r[:, :lanes]
    o_ref[1] = r[:, lanes:]


def project_q(x, w_query, groups):
    rows, width = x.shape
    lanes = w_query.shape[1] // groups
    return pl.pallas_call(
        project_q_kernel,
        grid=(groups // 2,),
        in_specs=[
            pl.BlockSpec((rows, width), lambda h: (0, 0)),
            pl.BlockSpec((width, lanes), lambda h: (0, 2 * h)),
            pl.BlockSpec((width, lanes), lambda h: (0, 2 * h + 1)),
        ],
        out_specs=pl.BlockSpec((2, rows, lanes), lambda h: (h, 0, 0)),
        out_shape=jax.ShapeDtypeStruct((groups, rows, lanes), jnp.bfloat16),
        cost_estimate=pl.CostEstimate(
            flops=2 * rows * width * w_query.shape[1],
            transcendentals=0,
            bytes_accessed=2 * width * w_query.shape[1] + 4 * rows * width,
        ),
        name="project_q",
    )(x, w_query, w_query)


def pick_kernel(index_ref, x_ref, *o_refs):
    count = x_ref.shape[0]

    def step(d, carry):
        for s, o_ref in enumerate(o_refs):
            o_ref[d] = x_ref[index_ref[s * count + d]]
        return carry

    lax.fori_loop(0, count, step, 0)


def pick_tiles(index, x, dests):
    whole = pl.BlockSpec(x.shape, lambda i, idx: (0, 0, 0))
    out = (dests,) + x.shape[1:]
    return pl.pallas_call(
        pick_kernel,
        grid_spec=pltpu.PrefetchScalarGridSpec(
            num_scalar_prefetch=1,
            grid=(1,),
            in_specs=[whole],
            out_specs=[pl.BlockSpec(out, lambda i, idx: (0, 0, 0))] * CAP,
        ),
        out_shape=[jax.ShapeDtypeStruct(out, x.dtype)] * CAP,
        cost_estimate=pl.CostEstimate(flops=0, transcendentals=0, bytes_accessed=4 * x.size * 2),
        name="pick_tiles",
    )(index, x)


def split_heads(q):
    first = lax.broadcasted_iota(jnp.int32, q.shape, 1) < HEAD_DIM
    zero = jnp.zeros_like(q)
    return jnp.concatenate([jnp.where(first, q, zero), jnp.where(first, zero, q)], axis=0)


def join_heads(both):
    half = both.shape[0] // 2
    shape = (half, 2 * HEAD_DIM)
    first = lax.broadcasted_iota(jnp.int32, shape, 1) < HEAD_DIM
    return jnp.where(
        first, jnp.broadcast_to(both[:half], shape), jnp.broadcast_to(both[half:], shape)
    )


def score(q2, keys):
    return lax.dot_general(q2, keys, (((1,), (1,)), ((), ())), preferred_element_type=jnp.float32)


def local_kernel(shard_ref, q_ref, kv_ref, before_ref, after_ref, global_ref, m_ref, l_ref, a_ref, pad_ref):
    tiles_here = kv_ref.shape[0] // TILE
    lanes = q_ref.shape[1]
    step = pl.program_id(0)
    per_step = q_ref.shape[0] // TILE

    @pl.when(step == 0)
    def _():
        pad_ref[0:TILE] = before_ref[...]
        pad_ref[TILE : TILE + kv_ref.shape[0]] = kv_ref[...]
        pad_ref[TILE + kv_ref.shape[0] :] = after_ref[...]

    tiles_total = shard_ref[1]
    for i in range(per_step):
        t = step * per_step + i
        rows = pl.ds(i * TILE, TILE)
        q2 = split_heads(q_ref[rows, :])
        window = pad_ref[pl.ds(pl.multiple_of(t * TILE, TILE), 3 * TILE), :]
        first_id = shard_ref[0] * tiles_here + t - 1
        position = lax.broadcasted_iota(jnp.int32, (2 * TILE, 3 * TILE), 1)
        ok = (position >= (GLOBALS - first_id) * TILE) & (
            position < (tiles_total - first_id) * TILE
        )
        s_window = jnp.where(ok, score(q2, window[:, :lanes]), NEG)
        s_global = score(q2, global_ref[:, :lanes])
        top = jnp.maximum(
            jnp.max(s_window, axis=1, keepdims=True), jnp.max(s_global, axis=1, keepdims=True)
        )
        p_window = jnp.exp2((s_window - top) * SCALE)
        p_global = jnp.exp2((s_global - top) * SCALE)
        total = jnp.sum(p_window, axis=1, keepdims=True) + jnp.sum(p_global, axis=1, keepdims=True)
        acc = jnp.dot(
            p_window.astype(jnp.bfloat16), window[:, lanes:], preferred_element_type=jnp.float32
        ) + jnp.dot(
            p_global.astype(jnp.bfloat16), global_ref[:, lanes:], preferred_element_type=jnp.float32
        )
        m_ref[rows, :] = join_heads(top)
        l_ref[rows, :] = join_heads(total)
        a_ref[rows, :] = join_heads(acc)


def local_attention(shard, q, kv, before, after, global_kv, per_step=2):
    rows, lanes = q.shape
    block = pl.BlockSpec((per_step * TILE, lanes), lambda i, s: (i, 0))
    fixed = lambda a: pl.BlockSpec(a.shape, lambda i, s: (0, 0))
    out = jax.ShapeDtypeStruct((rows, lanes), jnp.float32)
    keys = (3 + GLOBALS) * TILE
    return pl.pallas_call(
        local_kernel,
        grid_spec=pltpu.PrefetchScalarGridSpec(
            num_scalar_prefetch=1,
            grid=(rows // (per_step * TILE),),
            in_specs=[block, fixed(kv), fixed(before), fixed(after), fixed(global_kv)],
            out_specs=[block] * 3,
            scratch_shapes=[pltpu.VMEM((rows + 2 * TILE, 2 * lanes), jnp.bfloat16)],
        ),
        out_shape=[out] * 3,
        cost_estimate=pl.CostEstimate(
            flops=8 * rows * keys * lanes,
            transcendentals=2 * rows * keys,
            bytes_accessed=rows * lanes * 20,
        ),
        name="local_attention",
    )(shard, q, kv, before, after, global_kv)


def random_kernel(index_ref, count_ref, q_ref, kv0_ref, kv1_ref, kv2_ref, m_ref, l_ref, a_ref, o_ref, kv_ref):
    lanes = q_ref.shape[1]
    step = pl.program_id(0)
    per_step = q_ref.shape[0] // TILE
    parts = kv0_ref.shape[0]
    shards = kv0_ref.shape[1]
    part_rows = kv0_ref.shape[2]

    @pl.when(step == 0)
    def _():
        for s, ref in enumerate((kv0_ref, kv1_ref, kv2_ref)):
            for j in range(parts):
                kv_ref[s * shards : (s + 1) * shards, j * part_rows : (j + 1) * part_rows, :] = ref[j]

    for i in range(per_step):
        t = step * per_step + i
        rows = pl.ds(i * TILE, TILE)
        q2 = split_heads(q_ref[rows, :])
        count = count_ref[t]
        at = [index_ref[t * RANDOM + j] for j in range(RANDOM)]
        scores = []
        top = None
        for j in range(RANDOM):
            bias = jnp.where(j < count, 0.0, NEG).astype(jnp.float32)
            s = score(q2, kv_ref[at[j], :, :lanes]) + bias
            scores.append(s)
            top = s if top is None else jnp.maximum(top, s)
        m_old = m_ref[rows, :]
        m_old = jnp.concatenate([m_old[:, :1], m_old[:, HEAD_DIM : HEAD_DIM + 1]], axis=0)
        m_new = jnp.maximum(jnp.max(top, axis=1, keepdims=True), m_old)
        alpha = jnp.exp2((m_old - m_new) * SCALE)
        total = None
        acc = None
        for j in range(0, RANDOM, 2):
            p0 = jnp.exp2((scores[j] - m_new) * SCALE)
            p1 = jnp.exp2((scores[j + 1] - m_new) * SCALE)
            total = p0 + p1 if total is None else total + (p0 + p1)
            p = jnp.concatenate([p0.astype(jnp.bfloat16), p1.astype(jnp.bfloat16)], axis=1)
            v = jnp.concatenate([kv_ref[at[j], :, lanes:], kv_ref[at[j + 1], :, lanes:]], axis=0)
            part = jnp.dot(p, v, preferred_element_type=jnp.float32)
            acc = part if acc is None else acc + part
        alpha = join_heads(alpha)
        denominator = l_ref[rows, :] * alpha + join_heads(jnp.sum(total, axis=1, keepdims=True))
        numerator = a_ref[rows, :] * alpha + join_heads(acc)
        o_ref[rows, :] = (numerator / denominator).astype(jnp.bfloat16)


def random_attention(index, count, q, kvs, m, l, a, per_step=2):
    rows, lanes = q.shape
    parts, shards, part_rows, both = kvs[0].shape
    block = pl.BlockSpec((per_step * TILE, lanes), lambda i, s, c: (i, 0))
    fixed = pl.BlockSpec(kvs[0].shape, lambda i, s, c: (0, 0, 0, 0))
    keys = RANDOM * TILE
    return pl.pallas_call(
        random_kernel,
        grid_spec=pltpu.PrefetchScalarGridSpec(
            num_scalar_prefetch=2,
            grid=(rows // (per_step * TILE),),
            in_specs=[block] + [fixed] * CAP + [block] * 3,
            out_specs=block,
            scratch_shapes=[pltpu.VMEM((CAP * shards, parts * part_rows, both), jnp.bfloat16)],
        ),
        out_shape=jax.ShapeDtypeStruct((rows, lanes), jnp.bfloat16),
        cost_estimate=pl.CostEstimate(
            flops=8 * rows * keys * lanes,
            transcendentals=2 * rows * keys,
            bytes_accessed=rows * lanes * 16 + CAP * kvs[0].size * 2,
        ),
        name="random_attention",
    )(index, count, q, *kvs, m, l, a)


def request_tables(random_tiles, random_count, shard, ctx_count, tiles_here):
    slots = random_tiles.shape[1]
    live = jnp.arange(slots, dtype=jnp.int32)[None, :] < random_count[:, None]
    entries = jnp.where(live, random_tiles, -1).reshape(ctx_count, tiles_here * slots)
    mine = shard * tiles_here + jnp.arange(tiles_here, dtype=jnp.int32)
    owned = jnp.any(entries[:, :, None] == mine[None, None, :], axis=1)
    k = jnp.arange(tiles_here, dtype=jnp.int32)
    rank = jnp.sum((owned[:, None, :] & (k[None, None, :] < k[None, :, None])).astype(jnp.int32), axis=2)
    hit = owned[:, None, :] & (rank[:, None, :] == jnp.arange(CAP, dtype=jnp.int32)[None, :, None])
    send = jnp.sum(jnp.where(hit, k[None, None, :], 0), axis=2)
    wanted = lax.dynamic_index_in_dim(entries, shard, 0, keepdims=False)
    tiles = jnp.arange(ctx_count * tiles_here, dtype=jnp.int32)
    needed = jnp.any(wanted[:, None] == tiles[None, :], axis=0)
    owner = wanted // tiles_here
    lower = (
        needed[None, :]
        & (tiles[None, :] < wanted[:, None])
        & (tiles[None, :] >= (owner * tiles_here)[:, None])
    )
    slot = jnp.sum(lower.astype(jnp.int32), axis=1)
    read = jnp.where(wanted >= 0, slot * ctx_count + owner, 0)
    return send.T.reshape(-1), read


def body(tokens, w_query, w_key, w_value, w_out, random_tiles, random_count):
    groups = lax.axis_size("head")
    ctx_count = lax.axis_size("ctx")
    rows, width = tokens.shape
    own_tiles = rows // TILE
    part = TILE // groups
    tiles_here = own_tiles * groups
    shard = lax.axis_index("ctx").astype(jnp.int32)

    striped = tokens.reshape(own_tiles, groups, part, width).transpose(1, 0, 2, 3)
    striped = lax.all_to_all(striped, "head", split_axis=0, concat_axis=0, tiled=True)
    striped = striped.reshape(tiles_here, part, width)
    send, read = request_tables(random_tiles, random_count, shard, ctx_count, tiles_here)
    outgoing = pick_tiles(send, striped, ctx_count)

    kv = project_kv(tokens, w_key, w_value, groups)
    kv = lax.all_to_all(kv, "head", split_axis=0, concat_axis=0, tiled=True)
    kv = kv.reshape(rows * groups, -1)
    q = project_q(tokens, w_query, groups)
    q = lax.all_to_all(q, "head", split_axis=0, concat_axis=0, tiled=True)
    q = q.reshape(rows * groups, -1)

    fetched = []
    for slot in range(CAP):
        got = lax.all_to_all(outgoing[slot], "ctx", split_axis=0, concat_axis=0, tiled=True)
        got = project_kv(got.reshape(ctx_count * part, width), w_key, w_value, groups)
        got = lax.all_to_all(got, "head", split_axis=0, concat_axis=0, tiled=True)
        fetched.append(got.reshape(groups, ctx_count, part, -1))

    up = [(i, (i + 1) % ctx_count) for i in range(ctx_count - 1)]
    down = [(j, i) for i, j in up]
    before = lax.ppermute(kv[-TILE:], "ctx", up)
    after = lax.ppermute(kv[:TILE], "ctx", down)
    root = kv[: GLOBALS * TILE]
    global_kv = lax.psum(jnp.where(shard == 0, root, 0).astype(root.dtype), "ctx")

    place = jnp.stack([shard, jnp.int32(tiles_here * ctx_count)])
    m, l, a = local_attention(place, q, kv, before, after, global_kv)
    my_count = lax.dynamic_slice_in_dim(random_count, shard * tiles_here, tiles_here, 0)
    attended = random_attention(read, my_count, q, fetched, m, l, a)
    attended = attended.reshape(groups, rows, -1)
    returned = lax.all_to_all(attended, "head", split_axis=0, concat_axis=0, tiled=True)
    out = lax.dot_general(
        returned,
        w_out.reshape(groups, -1, width),
        (((0, 2), (0, 1)), ((), ())),
        preferred_element_type=jnp.float32,
    )
    return out.astype(jnp.bfloat16)


def solution(mesh):
    return jax.shard_map(
        body,
        mesh=mesh,
        in_specs=(P(("ctx", "head"), None), P(), P(), P(), P(), P(), P()),
        out_specs=P(("ctx", "head"), None),
        check_vma=False,
    )
```

```python
import functools

import jax
import jax.numpy as jnp
from jax import lax
from jax.experimental import pallas as pl
from jax.experimental.pallas import tpu as pltpu
from jax.sharding import PartitionSpec as P


HEAD_DIM = 64
TILE = 128
GLOBALS = 2
RANDOM = 12
CAP = 3
LOG2E = 1.4426950408889634
SCALE = HEAD_DIM ** (-0.5) * LOG2E
NEG = -1e30


def project_kernel(here_ref, *refs, sources, weights, groups):
    x_refs, rest = refs[:sources], refs[sources:]
    w_refs, o_refs, x_ref = rest[:weights], rest[weights : weights + groups], rest[-1]
    step = pl.program_id(0)

    @pl.when(step == 0)
    def _():
        row = 0
        for ref in x_refs:
            x_ref[row : row + ref.shape[0]] = ref[...]
            row += ref.shape[0]

    w = jnp.concatenate([ref[...] for ref in w_refs], axis=1)
    r = jnp.dot(x_ref[...], w, preferred_element_type=jnp.float32).astype(jnp.bfloat16)
    for o, o_ref in enumerate(o_refs):

        @pl.when(step == o)
        def _():
            o_ref[...] = r


def project(here, xs, ws, groups):
    rows = sum(x.shape[0] for x in xs)
    width = xs[0].shape[1]
    lanes = ws[0].shape[1] // groups
    out_lanes = lanes * len(ws)
    return pl.pallas_call(
        functools.partial(project_kernel, sources=len(xs), weights=len(ws), groups=groups),
        grid_spec=pltpu.PrefetchScalarGridSpec(
            num_scalar_prefetch=1,
            grid=(groups,),
            in_specs=[pl.BlockSpec(x.shape, lambda o, here: (0, 0)) for x in xs]
            + [
                pl.BlockSpec((width, lanes), lambda o, here: (0, lax.rem(here[0] + o, groups)))
                for _ in ws
            ],
            out_specs=[pl.BlockSpec((rows, out_lanes), lambda o, here: (0, 0))] * groups,
            scratch_shapes=[pltpu.VMEM((rows, width), jnp.bfloat16)],
        ),
        out_shape=[jax.ShapeDtypeStruct((rows, out_lanes), jnp.bfloat16)] * groups,
        cost_estimate=pl.CostEstimate(
            flops=2 * rows * width * lanes * len(ws) * groups,
            transcendentals=0,
            bytes_accessed=2 * width * lanes * len(ws) * groups + 2 * rows * (width + out_lanes * groups),
        ),
    )(here, *xs, *ws)


def exchange(pieces, axis):
    size = len(pieces)
    return [pieces[0]] + [
        lax.ppermute(pieces[o], axis, [(i, (i + o) % size) for i in range(size)])
        for o in range(1, size)
    ]


def broadcast_first(value, axis, index):
    size = lax.axis_size(axis)
    hop = size // 2
    while hop:
        got = lax.ppermute(value, axis, [(i, i + hop) for i in range(0, size, 2 * hop)])
        value = jnp.where(lax.rem(index, 2 * hop) == hop, got, value)
        hop //= 2
    return value


def pick_kernel(index_ref, x_ref, *o_refs):
    count = x_ref.shape[0]

    def step(d, carry):
        for s, o_ref in enumerate(o_refs):
            o_ref[d] = x_ref[index_ref[s * count + d]]
        return carry

    lax.fori_loop(0, count, step, 0)


def pick_tiles(index, x, dests):
    whole = pl.BlockSpec(x.shape, lambda i, idx: (0, 0, 0))
    out = (dests,) + x.shape[1:]
    return pl.pallas_call(
        pick_kernel,
        grid_spec=pltpu.PrefetchScalarGridSpec(
            num_scalar_prefetch=1,
            grid=(1,),
            in_specs=[whole],
            out_specs=[pl.BlockSpec(out, lambda i, idx: (0, 0, 0))] * CAP,
        ),
        out_shape=[jax.ShapeDtypeStruct(out, x.dtype)] * CAP,
        cost_estimate=pl.CostEstimate(flops=0, transcendentals=0, bytes_accessed=4 * x.size * 2),
        name="pick_tiles",
    )(index, x)


def split_heads(q):
    first = lax.broadcasted_iota(jnp.int32, q.shape, 1) < HEAD_DIM
    zero = jnp.zeros_like(q)
    return jnp.concatenate([jnp.where(first, q, zero), jnp.where(first, zero, q)], axis=0)


def join_heads(both):
    half = both.shape[0] // 2
    shape = (half, 2 * HEAD_DIM)
    first = lax.broadcasted_iota(jnp.int32, shape, 1) < HEAD_DIM
    return jnp.where(
        first, jnp.broadcast_to(both[:half], shape), jnp.broadcast_to(both[half:], shape)
    )


def score(q2, keys):
    return lax.dot_general(q2, keys, (((1,), (1,)), ((), ())), preferred_element_type=jnp.float32)


def local_kernel(place_ref, *refs, groups):
    own_refs, ext_refs = refs[:groups], refs[groups : 2 * groups]
    m_ref, l_ref, a_ref, qo_ref, q_ref, pad_ref = refs[2 * groups :]
    own_rows = own_refs[0].shape[0]
    part = ext_refs[0].shape[0] // (2 + GLOBALS)
    tiles_here = own_rows * groups // TILE
    lanes = m_ref.shape[1]
    step = pl.program_id(0)
    per_step = m_ref.shape[0] // TILE

    @pl.when(step == 0)
    def _():
        homes = [0] + [tiles_here + 1 + i for i in range(1 + GLOBALS)]
        for o in range(groups):
            row = pl.multiple_of(lax.rem(place_ref[2] + groups - o, groups) * own_rows, own_rows)
            q_ref[pl.ds(row, own_rows), :] = own_refs[o][:, :lanes]
            pad_ref[pl.ds(row + TILE, own_rows), :] = own_refs[o][:, lanes:]
            for i, home in enumerate(homes):
                row = home * TILE + o * part
                pad_ref[row : row + part, :] = ext_refs[o][i * part : (i + 1) * part, :]

    tiles_total = place_ref[1]
    global_kv = pad_ref[(tiles_here + 2) * TILE :, :]
    for i in range(per_step):
        t = step * per_step + i
        rows = pl.ds(i * TILE, TILE)
        q = q_ref[pl.ds(pl.multiple_of(t * TILE, TILE), TILE), :]
        q2 = split_heads(q)
        window = pad_ref[pl.ds(pl.multiple_of(t * TILE, TILE), 3 * TILE), :]
        first_id = place_ref[0] * tiles_here + t - 1
        position = lax.broadcasted_iota(jnp.int32, (2 * TILE, 3 * TILE), 1)
        ok = (position >= (GLOBALS - first_id) * TILE) & (
            position < (tiles_total - first_id) * TILE
        )
        s_window = jnp.where(ok, score(q2, window[:, :lanes]), NEG)
        s_global = score(q2, global_kv[:, :lanes])
        top = jnp.maximum(
            jnp.max(s_window, axis=1, keepdims=True), jnp.max(s_global, axis=1, keepdims=True)
        )
        p_window = jnp.exp2((s_window - top) * SCALE)
        p_global = jnp.exp2((s_global - top) * SCALE)
        total = jnp.sum(p_window, axis=1, keepdims=True) + jnp.sum(p_global, axis=1, keepdims=True)
        acc = jnp.dot(
            p_window.astype(jnp.bfloat16), window[:, lanes:], preferred_element_type=jnp.float32
        ) + jnp.dot(
            p_global.astype(jnp.bfloat16), global_kv[:, lanes:], preferred_element_type=jnp.float32
        )
        m_ref[rows, :] = join_heads(top)
        l_ref[rows, :] = join_heads(total)
        a_ref[rows, :] = join_heads(acc)
        qo_ref[rows, :] = q


def local_attention(place, own, ext, ext_rows, per_step=2):
    groups = len(own)
    rows = own[0].shape[0] * groups
    both = ext[0].shape[1]
    lanes = both // 2
    block = pl.BlockSpec((per_step * TILE, lanes), lambda i, s: (i, 0))
    last = ext[0].shape[0] // ext_rows - 1
    out = jax.ShapeDtypeStruct((rows, lanes), jnp.float32)
    keys = (3 + GLOBALS) * TILE
    return pl.pallas_call(
        functools.partial(local_kernel, groups=groups),
        grid_spec=pltpu.PrefetchScalarGridSpec(
            num_scalar_prefetch=1,
            grid=(rows // (per_step * TILE),),
            in_specs=[pl.BlockSpec(a.shape, lambda i, s: (0, 0)) for a in own]
            + [pl.BlockSpec((ext_rows, both), lambda i, s: (last, 0)) for _ in ext],
            out_specs=[block] * 4,
            scratch_shapes=[
                pltpu.VMEM((rows, lanes), jnp.bfloat16),
                pltpu.VMEM((rows + (2 + GLOBALS) * TILE, both), jnp.bfloat16),
            ],
        ),
        out_shape=[out] * 3 + [jax.ShapeDtypeStruct((rows, lanes), jnp.bfloat16)],
        cost_estimate=pl.CostEstimate(
            flops=8 * rows * keys * lanes,
            transcendentals=2 * rows * keys,
            bytes_accessed=rows * lanes * 20,
        ),
        name="local_attention",
    )(place, *own, *ext)


def random_kernel(index_ref, count_ref, *refs, groups):
    part_refs = refs[: CAP * groups]
    q_ref, m_ref, l_ref, a_ref, o_ref, kv_ref = refs[CAP * groups :]
    lanes = q_ref.shape[1]
    step = pl.program_id(0)
    per_step = q_ref.shape[0] // TILE
    part = TILE // groups
    shards = part_refs[0].shape[0] // part

    @pl.when(step == 0)
    def _():
        for i, ref in enumerate(part_refs):
            s, o = divmod(i, groups)
            kv_ref[s * shards : (s + 1) * shards, o * part : (o + 1) * part, :] = ref[...].reshape(
                shards, part, 2 * lanes
            )

    for i in range(per_step):
        t = step * per_step + i
        rows = pl.ds(i * TILE, TILE)
        q2 = split_heads(q_ref[rows, :])
        count = count_ref[t]
        at = [index_ref[t * RANDOM + j] for j in range(RANDOM)]
        scores = []
        top = None
        for j in range(RANDOM):
            bias = jnp.where(j < count, 0.0, NEG).astype(jnp.float32)
            s = score(q2, kv_ref[at[j], :, :lanes]) + bias
            scores.append(s)
            top = s if top is None else jnp.maximum(top, s)
        m_old = m_ref[rows, :]
        m_old = jnp.concatenate([m_old[:, :1], m_old[:, HEAD_DIM : HEAD_DIM + 1]], axis=0)
        m_new = jnp.maximum(jnp.max(top, axis=1, keepdims=True), m_old)
        alpha = jnp.exp2((m_old - m_new) * SCALE)
        total = None
        acc = None
        for j in range(0, RANDOM, 2):
            p0 = jnp.exp2((scores[j] - m_new) * SCALE)
            p1 = jnp.exp2((scores[j + 1] - m_new) * SCALE)
            total = p0 + p1 if total is None else total + (p0 + p1)
            p = jnp.concatenate([p0.astype(jnp.bfloat16), p1.astype(jnp.bfloat16)], axis=1)
            v = jnp.concatenate([kv_ref[at[j], :, lanes:], kv_ref[at[j + 1], :, lanes:]], axis=0)
            part = jnp.dot(p, v, preferred_element_type=jnp.float32)
            acc = part if acc is None else acc + part
        alpha = join_heads(alpha)
        denominator = l_ref[rows, :] * alpha + join_heads(jnp.sum(total, axis=1, keepdims=True))
        numerator = a_ref[rows, :] * alpha + join_heads(acc)
        o_ref[rows, :] = (numerator / denominator).astype(jnp.bfloat16)


def random_attention(index, count, q, fetched, m, l, a, part_rows, per_step=2):
    rows, lanes = q.shape
    groups = len(fetched) // CAP
    block = pl.BlockSpec((per_step * TILE, lanes), lambda i, s, c: (i, 0))
    fixed = pl.BlockSpec((part_rows, 2 * lanes), lambda i, s, c: (0, 0))
    keys = RANDOM * TILE
    return pl.pallas_call(
        functools.partial(random_kernel, groups=groups),
        grid_spec=pltpu.PrefetchScalarGridSpec(
            num_scalar_prefetch=2,
            grid=(rows // (per_step * TILE),),
            in_specs=[fixed] * len(fetched) + [block] * 4,
            out_specs=block,
            scratch_shapes=[
                pltpu.VMEM((CAP * part_rows * groups // TILE, TILE, 2 * lanes), jnp.bfloat16)
            ],
        ),
        out_shape=jax.ShapeDtypeStruct((rows, lanes), jnp.bfloat16),
        cost_estimate=pl.CostEstimate(
            flops=8 * rows * keys * lanes,
            transcendentals=2 * rows * keys,
            bytes_accessed=rows * lanes * 16 + CAP * part_rows * groups * lanes * 4,
        ),
        name="random_attention",
    )(index, count, *fetched, q, m, l, a)


def request_tables(random_tiles, random_count, shard, ctx_count, tiles_here):
    slots = random_tiles.shape[1]
    live = jnp.arange(slots, dtype=jnp.int32)[None, :] < random_count[:, None]
    entries = jnp.where(live, random_tiles, -1).reshape(ctx_count, tiles_here * slots)
    mine = shard * tiles_here + jnp.arange(tiles_here, dtype=jnp.int32)
    owned = jnp.any(entries[:, :, None] == mine[None, None, :], axis=1)
    k = jnp.arange(tiles_here, dtype=jnp.int32)
    rank = jnp.sum((owned[:, None, :] & (k[None, None, :] < k[None, :, None])).astype(jnp.int32), axis=2)
    hit = owned[:, None, :] & (rank[:, None, :] == jnp.arange(CAP, dtype=jnp.int32)[None, :, None])
    send = jnp.sum(jnp.where(hit, k[None, None, :], 0), axis=2)
    wanted = lax.dynamic_index_in_dim(entries, shard, 0, keepdims=False)
    tiles = jnp.arange(ctx_count * tiles_here, dtype=jnp.int32)
    needed = jnp.any(wanted[:, None] == tiles[None, :], axis=0)
    owner = wanted // tiles_here
    lower = (
        needed[None, :]
        & (tiles[None, :] < wanted[:, None])
        & (tiles[None, :] >= (owner * tiles_here)[:, None])
    )
    slot = jnp.sum(lower.astype(jnp.int32), axis=1)
    read = jnp.where(wanted >= 0, slot * ctx_count + owner, 0)
    return send.T.reshape(-1), read


def body(tokens, w_query, w_key, w_value, w_out, random_tiles, random_count):
    groups = lax.axis_size("head")
    ctx_count = lax.axis_size("ctx")
    rows, width = tokens.shape
    own_tiles = rows // TILE
    part = TILE // groups
    tiles_here = own_tiles * groups
    shard = lax.axis_index("ctx").astype(jnp.int32)

    here = lax.axis_index("head").astype(jnp.int32)

    striped = tokens.reshape(own_tiles, groups, part, width).transpose(1, 0, 2, 3)
    striped = lax.all_to_all(striped, "head", split_axis=0, concat_axis=0, tiled=True)
    striped = striped.reshape(tiles_here, part, width)
    send, read = request_tables(random_tiles, random_count, shard, ctx_count, tiles_here)
    outgoing = pick_tiles(send, striped, ctx_count)

    where = here[None]
    own = project(where, [tokens], [w_query, w_key, w_value], groups)
    own = exchange(own, "head")

    up = [(i, i + 1) for i in range(ctx_count - 1)]
    down = [(j, i) for i, j in up]
    before = lax.ppermute(striped[-1:], "ctx", up)
    after = lax.ppermute(striped[:1], "ctx", down)
    root = broadcast_first(striped[:GLOBALS], "ctx", shard)
    ext = jnp.concatenate([before, after, root], axis=0).reshape(-1, width)

    fetched = []
    for slot in range(CAP):
        got = lax.all_to_all(outgoing[slot], "ctx", split_axis=0, concat_axis=0, tiled=True)
        got = [got.reshape(ctx_count * part, width)] + ([ext] if slot == 0 else [])
        got = project(where, got, [w_key, w_value], groups)
        fetched += exchange(got, "head")

    place = jnp.stack([shard, jnp.int32(tiles_here * ctx_count), here])
    m, l, a, q = local_attention(place, own, fetched[:groups], ext.shape[0])
    my_count = lax.dynamic_slice_in_dim(random_count, shard * tiles_here, tiles_here, 0)
    attended = random_attention(read, my_count, q, fetched, m, l, a, ctx_count * part)
    attended = attended.reshape(groups, rows, -1)
    returned = lax.all_to_all(attended, "head", split_axis=0, concat_axis=0, tiled=True)
    out = lax.dot_general(
        returned,
        w_out.reshape(groups, -1, width),
        (((0, 2), (0, 1)), ((), ())),
        preferred_element_type=jnp.float32,
    )
    return out.astype(jnp.bfloat16)


def solution(mesh):
    return jax.shard_map(
        body,
        mesh=mesh,
        in_specs=(P(("ctx", "head"), None), P(), P(), P(), P(), P(), P()),
        out_specs=P(("ctx", "head"), None),
        check_vma=False,
    )
```

```python
import functools

import jax
import jax.numpy as jnp
from jax import lax
from jax.experimental import pallas as pl
from jax.experimental.pallas import tpu as pltpu
from jax.sharding import PartitionSpec as P


HEAD_DIM = 64
TILE = 128
GLOBALS = 2
RANDOM = 12
CAP = 3
LOG2E = 1.4426950408889634
SCALE = HEAD_DIM ** (-0.5) * LOG2E
NEG = -1e30


def project_kernel(here_ref, *refs, sources, weights, groups):
    x_refs, rest = refs[:sources], refs[sources:]
    w_refs, o_refs, x_ref = rest[:weights], rest[weights : weights + groups], rest[-1]
    step = pl.program_id(0)

    @pl.when(step == 0)
    def _():
        row = 0
        for ref in x_refs:
            x_ref[row : row + ref.shape[0]] = ref[...]
            row += ref.shape[0]

    w = jnp.concatenate([ref[...] for ref in w_refs], axis=1)
    r = jnp.dot(x_ref[...], w, preferred_element_type=jnp.float32).astype(jnp.bfloat16)
    for o, o_ref in enumerate(o_refs):

        @pl.when(step == o)
        def _():
            o_ref[...] = r


def project(here, xs, ws, groups):
    rows = sum(x.shape[0] for x in xs)
    width = xs[0].shape[1]
    lanes = ws[0].shape[1] // groups
    out_lanes = lanes * len(ws)
    return pl.pallas_call(
        functools.partial(project_kernel, sources=len(xs), weights=len(ws), groups=groups),
        grid_spec=pltpu.PrefetchScalarGridSpec(
            num_scalar_prefetch=1,
            grid=(groups,),
            in_specs=[pl.BlockSpec(x.shape, lambda o, here: (0, 0)) for x in xs]
            + [
                pl.BlockSpec((width, lanes), lambda o, here: (0, lax.rem(here[0] + o, groups)))
                for _ in ws
            ],
            out_specs=[pl.BlockSpec((rows, out_lanes), lambda o, here: (0, 0))] * groups,
            scratch_shapes=[pltpu.VMEM((rows, width), jnp.bfloat16)],
        ),
        out_shape=[jax.ShapeDtypeStruct((rows, out_lanes), jnp.bfloat16)] * groups,
        cost_estimate=pl.CostEstimate(
            flops=2 * rows * width * lanes * len(ws) * groups,
            transcendentals=0,
            bytes_accessed=2 * width * lanes * len(ws) * groups + 2 * rows * (width + out_lanes * groups),
        ),
    )(here, *xs, *ws)


def exchange(pieces, axis):
    size = len(pieces)
    return [pieces[0]] + [
        lax.ppermute(pieces[o], axis, [(i, (i + o) % size) for i in range(size)])
        for o in range(1, size)
    ]


def broadcast_first(value, axis, index):
    size = lax.axis_size(axis)
    hop, level = size // 2, 0
    while hop:
        got = lax.ppermute(value, axis, [(i, i + hop) for i in range(0, size, 2 * hop)])
        value = jnp.where(lax.rem(index, 2 * hop) == hop, got, value)
        hop //= 2
        level += 1
    return value


def pick_kernel(index_ref, x_ref, *o_refs):
    count = x_ref.shape[0]

    def step(d, carry):
        for s, o_ref in enumerate(o_refs):
            o_ref[d] = x_ref[index_ref[s * count + d]]
        return carry

    lax.fori_loop(0, count, step, 0)


def pick_tiles(index, x, dests):
    whole = pl.BlockSpec(x.shape, lambda i, idx: (0, 0, 0))
    out = (dests,) + x.shape[1:]
    return pl.pallas_call(
        pick_kernel,
        grid_spec=pltpu.PrefetchScalarGridSpec(
            num_scalar_prefetch=1,
            grid=(1,),
            in_specs=[whole],
            out_specs=[pl.BlockSpec(out, lambda i, idx: (0, 0, 0))] * CAP,
        ),
        out_shape=[jax.ShapeDtypeStruct(out, x.dtype)] * CAP,
        cost_estimate=pl.CostEstimate(flops=0, transcendentals=0, bytes_accessed=4 * x.size * 2),
        name="pick_tiles",
    )(index, x)


def split_heads(q):
    first = lax.broadcasted_iota(jnp.int32, q.shape, 1) < HEAD_DIM
    zero = jnp.zeros_like(q)
    return jnp.concatenate([jnp.where(first, q, zero), jnp.where(first, zero, q)], axis=0)


def join_heads(both):
    half = both.shape[0] // 2
    shape = (half, 2 * HEAD_DIM)
    first = lax.broadcasted_iota(jnp.int32, shape, 1) < HEAD_DIM
    return jnp.where(
        first, jnp.broadcast_to(both[:half], shape), jnp.broadcast_to(both[half:], shape)
    )


def score(q2, keys):
    return lax.dot_general(q2, keys, (((1,), (1,)), ((), ())), preferred_element_type=jnp.float32)


def local_kernel(place_ref, *refs, groups):
    own_refs, ext_refs = refs[:groups], refs[groups : 2 * groups]
    m_ref, l_ref, a_ref, qo_ref, q_ref, pad_ref = refs[2 * groups :]
    own_rows = own_refs[0].shape[0]
    part = ext_refs[0].shape[0] // (2 + GLOBALS)
    tiles_here = own_rows * groups // TILE
    lanes = m_ref.shape[1]
    step = pl.program_id(0)
    per_step = m_ref.shape[0] // TILE

    @pl.when(step == 0)
    def _():
        homes = [0] + [tiles_here + 1 + i for i in range(1 + GLOBALS)]
        for o in range(groups):
            row = pl.multiple_of(lax.rem(place_ref[2] + groups - o, groups) * own_rows, own_rows)
            q_ref[pl.ds(row, own_rows), :] = own_refs[o][:, :lanes]
            pad_ref[pl.ds(row + TILE, own_rows), :] = own_refs[o][:, lanes:]
            for i, home in enumerate(homes):
                row = home * TILE + o * part
                pad_ref[row : row + part, :] = ext_refs[o][i * part : (i + 1) * part, :]

    tiles_total = place_ref[1]
    global_kv = pad_ref[(tiles_here + 2) * TILE :, :]
    for i in range(per_step):
        t = step * per_step + i
        rows = pl.ds(i * TILE, TILE)
        q = q_ref[pl.ds(pl.multiple_of(t * TILE, TILE), TILE), :]
        q2 = split_heads(q)
        window = pad_ref[pl.ds(pl.multiple_of(t * TILE, TILE), 3 * TILE), :]
        first_id = place_ref[0] * tiles_here + t - 1
        position = lax.broadcasted_iota(jnp.int32, (2 * TILE, 3 * TILE), 1)
        ok = (position >= (GLOBALS - first_id) * TILE) & (
            position < (tiles_total - first_id) * TILE
        )
        s_window = jnp.where(ok, score(q2, window[:, :lanes]), NEG)
        s_global = score(q2, global_kv[:, :lanes])
        top = jnp.maximum(
            jnp.max(s_window, axis=1, keepdims=True), jnp.max(s_global, axis=1, keepdims=True)
        )
        p_window = jnp.exp2((s_window - top) * SCALE)
        p_global = jnp.exp2((s_global - top) * SCALE)
        total = jnp.sum(p_window, axis=1, keepdims=True) + jnp.sum(p_global, axis=1, keepdims=True)
        acc = jnp.dot(
            p_window.astype(jnp.bfloat16), window[:, lanes:], preferred_element_type=jnp.float32
        ) + jnp.dot(
            p_global.astype(jnp.bfloat16), global_kv[:, lanes:], preferred_element_type=jnp.float32
        )
        m_ref[rows, :] = join_heads(top)
        l_ref[rows, :] = join_heads(total)
        a_ref[rows, :] = join_heads(acc)
        qo_ref[rows, :] = q


def local_attention(place, own, ext, ext_rows, per_step=2):
    groups = len(own)
    rows = own[0].shape[0] * groups
    both = ext[0].shape[1]
    lanes = both // 2
    block = pl.BlockSpec((per_step * TILE, lanes), lambda i, s: (i, 0))
    last = ext[0].shape[0] // ext_rows - 1
    out = jax.ShapeDtypeStruct((rows, lanes), jnp.float32)
    keys = (3 + GLOBALS) * TILE
    return pl.pallas_call(
        functools.partial(local_kernel, groups=groups),
        grid_spec=pltpu.PrefetchScalarGridSpec(
            num_scalar_prefetch=1,
            grid=(rows // (per_step * TILE),),
            in_specs=[pl.BlockSpec(a.shape, lambda i, s: (0, 0)) for a in own]
            + [pl.BlockSpec((ext_rows, both), lambda i, s: (last, 0)) for _ in ext],
            out_specs=[block] * 4,
            scratch_shapes=[
                pltpu.VMEM((rows, lanes), jnp.bfloat16),
                pltpu.VMEM((rows + (2 + GLOBALS) * TILE, both), jnp.bfloat16),
            ],
        ),
        out_shape=[out] * 3 + [jax.ShapeDtypeStruct((rows, lanes), jnp.bfloat16)],
        cost_estimate=pl.CostEstimate(
            flops=8 * rows * keys * lanes,
            transcendentals=2 * rows * keys,
            bytes_accessed=rows * lanes * 20,
        ),
        name="local_attention",
    )(place, *own, *ext)


def assemble_kernel(*refs):
    part_refs, (o_ref, sems) = refs[:-2], refs[-2:]
    shards, part = o_ref.shape[0], o_ref.shape[1] // len(part_refs)
    copies = [
        pltpu.make_async_copy(
            ref.at[:shards], o_ref.at[:, o * part : (o + 1) * part, :], sems.at[o]
        )
        for o, ref in enumerate(part_refs)
    ]
    for copy in copies:
        copy.start()
    for copy in copies:
        copy.wait()


def assemble(parts, shards):
    part = TILE // len(parts)
    lanes = parts[0].shape[1]
    return pl.pallas_call(
        assemble_kernel,
        in_specs=[pl.BlockSpec(memory_space=pl.ANY)] * len(parts),
        out_specs=pl.BlockSpec(memory_space=pl.ANY),
        out_shape=jax.ShapeDtypeStruct((shards, TILE, lanes), jnp.bfloat16),
        scratch_shapes=[pltpu.SemaphoreType.DMA((len(parts),))],
        cost_estimate=pl.CostEstimate(
            flops=0, transcendentals=0, bytes_accessed=4 * shards * TILE * lanes
        ),
    )(*[p.reshape(-1, part, lanes) for p in parts])


def random_kernel(index_ref, count_ref, *refs, groups):
    early_refs, part_refs = refs[: CAP - 1], refs[CAP - 1 : CAP - 1 + groups]
    q_ref, m_ref, l_ref, a_ref, o_ref, kv_ref, sems = refs[CAP - 1 + groups :]
    lanes = q_ref.shape[1]
    step = pl.program_id(0)
    per_step = q_ref.shape[0] // TILE
    part = TILE // groups
    shards = kv_ref.shape[0] // CAP

    @pl.when(step == 0)
    def _():
        copies = []
        for s, ref in enumerate(early_refs):
            home = kv_ref.at[s * shards : (s + 1) * shards]
            copies.append(pltpu.make_async_copy(ref, home, sems.at[s]))
        for o, ref in enumerate(part_refs):
            home = kv_ref.at[(CAP - 1) * shards :, o * part : (o + 1) * part, :]
            copies.append(pltpu.make_async_copy(ref, home, sems.at[CAP - 1 + o]))
        for copy in copies:
            copy.start()
        for copy in copies:
            copy.wait()

    for i in range(per_step):
        t = step * per_step + i
        rows = pl.ds(i * TILE, TILE)
        q2 = split_heads(q_ref[rows, :])
        count = count_ref[t]
        at = [index_ref[t * RANDOM + j] for j in range(RANDOM)]
        scores = []
        top = None
        for j in range(0, RANDOM, 2):
            keys = jnp.concatenate([kv_ref[at[j], :, :lanes], kv_ref[at[j + 1], :, :lanes]], axis=0)
            s = score(q2, keys)
            for i, part in enumerate((s[:, :TILE], s[:, TILE:])):
                part = part + jnp.where(j + i < count, 0.0, NEG).astype(jnp.float32)
                scores.append(part)
                top = part if top is None else jnp.maximum(top, part)
        m_old = m_ref[rows, :]
        m_old = jnp.concatenate([m_old[:, :1], m_old[:, HEAD_DIM : HEAD_DIM + 1]], axis=0)
        m_new = jnp.maximum(jnp.max(top, axis=1, keepdims=True), m_old)
        alpha = jnp.exp2((m_old - m_new) * SCALE)
        total = None
        acc = None
        for j in range(0, RANDOM, 2):
            p0 = jnp.exp2((scores[j] - m_new) * SCALE)
            p1 = jnp.exp2((scores[j + 1] - m_new) * SCALE)
            total = p0 + p1 if total is None else total + (p0 + p1)
            p = jnp.concatenate([p0.astype(jnp.bfloat16), p1.astype(jnp.bfloat16)], axis=1)
            v = jnp.concatenate([kv_ref[at[j], :, lanes:], kv_ref[at[j + 1], :, lanes:]], axis=0)
            part = jnp.dot(p, v, preferred_element_type=jnp.float32)
            acc = part if acc is None else acc + part
        alpha = join_heads(alpha)
        denominator = l_ref[rows, :] * alpha + join_heads(jnp.sum(total, axis=1, keepdims=True))
        numerator = a_ref[rows, :] * alpha + join_heads(acc)
        o_ref[rows, :] = (numerator / denominator).astype(jnp.bfloat16)


def random_attention(index, count, q, early, late, m, l, a, per_step=8):
    rows, lanes = q.shape
    groups = len(late)
    shards = early[0].shape[0]
    part = TILE // groups
    late = [f.reshape(-1, part, 2 * lanes) for f in late]
    block = pl.BlockSpec((per_step * TILE, lanes), lambda i, s, c: (i, 0))
    keys = RANDOM * TILE
    return pl.pallas_call(
        functools.partial(random_kernel, groups=groups),
        grid_spec=pltpu.PrefetchScalarGridSpec(
            num_scalar_prefetch=2,
            grid=(rows // (per_step * TILE),),
            in_specs=[pl.BlockSpec(memory_space=pl.ANY)] * (len(early) + groups) + [block] * 4,
            out_specs=block,
            scratch_shapes=[
                pltpu.VMEM((CAP * shards, TILE, 2 * lanes), jnp.bfloat16),
                pltpu.SemaphoreType.DMA((len(early) + groups,)),
            ],
        ),
        out_shape=jax.ShapeDtypeStruct((rows, lanes), jnp.bfloat16),
        cost_estimate=pl.CostEstimate(
            flops=8 * rows * keys * lanes,
            transcendentals=2 * rows * keys,
            bytes_accessed=rows * lanes * 16 + CAP * shards * TILE * lanes * 4,
        ),
        name="random_attention",
    )(index, count, *early, *late, q, m, l, a)


def request_tables(random_tiles, random_count, shard, ctx_count, tiles_here):
    slots = random_tiles.shape[1]
    live = jnp.arange(slots, dtype=jnp.int32)[None, :] < random_count[:, None]
    entries = jnp.where(live, random_tiles, -1).reshape(ctx_count, tiles_here * slots)
    mine = shard * tiles_here + jnp.arange(tiles_here, dtype=jnp.int32)
    owned = jnp.any(entries[:, :, None] == mine[None, None, :], axis=1)
    k = jnp.arange(tiles_here, dtype=jnp.int32)
    rank = jnp.sum((owned[:, None, :] & (k[None, None, :] < k[None, :, None])).astype(jnp.int32), axis=2)
    hit = owned[:, None, :] & (rank[:, None, :] == jnp.arange(CAP, dtype=jnp.int32)[None, :, None])
    send = jnp.sum(jnp.where(hit, k[None, None, :], 0), axis=2)
    wanted = lax.dynamic_index_in_dim(entries, shard, 0, keepdims=False)
    tiles = jnp.arange(ctx_count * tiles_here, dtype=jnp.int32)
    needed = jnp.any(wanted[:, None] == tiles[None, :], axis=0)
    owner = wanted // tiles_here
    lower = (
        needed[None, :]
        & (tiles[None, :] < wanted[:, None])
        & (tiles[None, :] >= (owner * tiles_here)[:, None])
    )
    slot = jnp.sum(lower.astype(jnp.int32), axis=1)
    read = jnp.where(wanted >= 0, slot * ctx_count + owner, 0)
    return send.T.reshape(-1), read


def body(tokens, w_query, w_key, w_value, w_out, random_tiles, random_count):
    groups = lax.axis_size("head")
    ctx_count = lax.axis_size("ctx")
    rows, width = tokens.shape
    own_tiles = rows // TILE
    part = TILE // groups
    tiles_here = own_tiles * groups
    shard = lax.axis_index("ctx").astype(jnp.int32)

    here = lax.axis_index("head").astype(jnp.int32)

    striped = tokens.reshape(own_tiles, groups, part, width).transpose(1, 0, 2, 3)
    striped = lax.all_to_all(striped, "head", split_axis=0, concat_axis=0, tiled=True)
    striped = striped.reshape(tiles_here, part, width)
    send, read = request_tables(random_tiles, random_count, shard, ctx_count, tiles_here)
    outgoing = pick_tiles(send, striped, ctx_count)

    where = here[None]
    own = project(where, [tokens], [w_query, w_key, w_value], groups)
    own = exchange(own, "head")

    up = [(i, i + 1) for i in range(ctx_count - 1)]
    down = [(j, i) for i, j in up]
    before = lax.ppermute(striped[-1:], "ctx", up)
    after = lax.ppermute(striped[:1], "ctx", down)
    root = broadcast_first(striped[:GLOBALS], "ctx", shard)
    ext = jnp.concatenate([before, after, root], axis=0).reshape(-1, width)

    fetched = []
    for slot in range(CAP):
        got = lax.all_to_all(outgoing[slot], "ctx", split_axis=0, concat_axis=0, tiled=True)
        got = [got.reshape(ctx_count * part, width)] + ([ext] if slot == 1 else [])
        got = project(where, got, [w_key, w_value], groups)
        fetched.append(exchange(got, "head"))

    place = jnp.stack([shard, jnp.int32(tiles_here * ctx_count), here])
    m, l, a, q = local_attention(place, own, fetched[1], ext.shape[0])
    early = []
    for slot in range(CAP - 1):
        early.append(assemble(fetched[slot], ctx_count))
    my_count = lax.dynamic_slice_in_dim(random_count, shard * tiles_here, tiles_here, 0)
    attended = random_attention(read, my_count, q, early, fetched[CAP - 1], m, l, a)
    attended = attended.reshape(groups, rows, -1)
    returned = lax.all_to_all(attended, "head", split_axis=0, concat_axis=0, tiled=True)
    out = lax.dot_general(
        returned,
        w_out.reshape(groups, -1, width),
        (((0, 2), (0, 1)), ((), ())),
        preferred_element_type=jnp.float32,
    )
    return out.astype(jnp.bfloat16)


def solution(mesh):
    return jax.shard_map(
        body,
        mesh=mesh,
        in_specs=(P(("ctx", "head"), None), P(), P(), P(), P(), P(), P()),
        out_specs=P(("ctx", "head"), None),
        check_vma=False,
    )
```

```python
import functools

import jax
import jax.numpy as jnp
from jax import lax
from jax.experimental import pallas as pl
from jax.experimental.pallas import tpu as pltpu
from jax.sharding import PartitionSpec as P


HEAD_DIM = 64
TILE = 128
GLOBALS = 2
RANDOM = 12
CAP = 3
LOG2E = 1.4426950408889634
SCALE = HEAD_DIM ** (-0.5) * LOG2E
NEG = -1e30
LANES = 128
SUB = 8


def project_kernel(here_ref, *refs, sources, weights, groups, place):
    x_refs, rest = refs[:sources], refs[sources:]
    w_refs, o_refs, x_ref = rest[:weights], rest[weights : weights + groups], rest[-1]
    step = pl.program_id(0)

    @pl.when(step == 0)
    def _():
        place(x_ref, *x_refs)

    w = jnp.concatenate([ref[...] for ref in w_refs], axis=1)
    r = jnp.dot(x_ref[...], w, preferred_element_type=jnp.float32).astype(jnp.bfloat16)
    for o, o_ref in enumerate(o_refs):

        @pl.when(step == o)
        def _():
            o_ref[...] = r


def place_rows(x_ref, rows_ref):
    x_ref[...] = rows_ref[...]


def place_chunks(x_ref, got_ref):
    shards, _, lanes = got_ref.shape
    part = x_ref.shape[0] // shards
    for k in range(x_ref.shape[1] // lanes):
        x_ref[:, k * lanes : (k + 1) * lanes] = got_ref[:, k * part : (k + 1) * part, :].reshape(
            shards * part, lanes
        )


def place_chunks_and_edges(x_ref, got_ref, edge_ref):
    shards, tall, lanes = got_ref.shape
    edges = edge_ref.shape[0]
    width = x_ref.shape[1]
    across = width // lanes
    extra = shards * SUB // across
    rows = x_ref.shape[0] - edges - extra
    place_chunks(x_ref.at[:rows], got_ref)
    x_ref[rows : rows + edges] = edge_ref[...]
    for b in range(shards):
        row = rows + edges + b // across * SUB
        lane = b % across * lanes
        x_ref[row : row + SUB, lane : lane + lanes] = got_ref[b, tall - SUB :, :]


def project(here, xs, rows, ws, groups, place):
    width = ws[0].shape[0]
    lanes = ws[0].shape[1] // groups
    out_lanes = lanes * len(ws)
    return pl.pallas_call(
        functools.partial(
            project_kernel, sources=len(xs), weights=len(ws), groups=groups, place=place
        ),
        grid_spec=pltpu.PrefetchScalarGridSpec(
            num_scalar_prefetch=1,
            grid=(groups,),
            in_specs=[
                pl.BlockSpec(x.shape, lambda o, here, n=len(x.shape): (0,) * n) for x in xs
            ]
            + [
                pl.BlockSpec((width, lanes), lambda o, here: (0, lax.rem(here[0] + o, groups)))
                for _ in ws
            ],
            out_specs=[pl.BlockSpec((rows, out_lanes), lambda o, here: (0, 0))] * groups,
            scratch_shapes=[pltpu.VMEM((rows, width), jnp.bfloat16)],
        ),
        out_shape=[jax.ShapeDtypeStruct((rows, out_lanes), jnp.bfloat16)] * groups,
        cost_estimate=pl.CostEstimate(
            flops=2 * rows * width * lanes * len(ws) * groups,
            transcendentals=0,
            bytes_accessed=2 * width * lanes * len(ws) * groups + 2 * rows * (width + out_lanes * groups),
        ),
    )(here, *xs, *ws)


def exchange(pieces, axis):
    size = len(pieces)
    return [pieces[0]] + [
        lax.ppermute(pieces[o], axis, [(i, (i + o) % size) for i in range(size)])
        for o in range(1, size)
    ]


def pick_chunk(o_ref, d, tile):
    lanes = o_ref.shape[2]
    part, width = tile.shape
    for k in range(width // lanes):
        o_ref[d, k * part : (k + 1) * part, :] = tile[:, k * lanes : (k + 1) * lanes]


def pick_first_kernel(index_ref, x_ref, o_ref):
    dests, tall, lanes = o_ref.shape
    part, width = x_ref.shape[1:]
    across = width // lanes

    def step(d, carry):
        pick_chunk(o_ref, d, x_ref[index_ref[d]])
        return carry

    lax.fori_loop(0, dests, step, 0)
    for b in range(dests):
        row = b // across * SUB
        lane = b % across * lanes
        o_ref[b, tall - SUB :, :] = x_ref[
            row // part, row % part : row % part + SUB, lane : lane + lanes
        ]


def pick_second_kernel(index_ref, x_ref, root_ref, o_ref):
    dests, tall, _ = o_ref.shape
    block = root_ref[0]

    def step(d, carry):
        pick_chunk(o_ref, d, x_ref[index_ref[d]])
        o_ref[d, tall - SUB :, :] = block
        return carry

    lax.fori_loop(0, dests, step, 0)


def pick_chunks(index, x, dests, got):
    _, part, width = x.shape
    tall = part * width // LANES + SUB
    out = (dests, tall, LANES)
    whole = lambda shape: pl.BlockSpec(shape, lambda i, idx: (0,) * len(shape))
    ins, specs, kernel = [x], [whole(x.shape)], pick_first_kernel
    if got is not None:
        ins.append(got)
        specs.append(pl.BlockSpec((1, SUB, LANES), lambda i, idx: (0, tall // SUB - 1, 0)))
        kernel = pick_second_kernel
    return pl.pallas_call(
        kernel,
        grid_spec=pltpu.PrefetchScalarGridSpec(
            num_scalar_prefetch=1, grid=(1,), in_specs=specs, out_specs=whole(out)
        ),
        out_shape=jax.ShapeDtypeStruct(out, x.dtype),
        cost_estimate=pl.CostEstimate(flops=0, transcendentals=0, bytes_accessed=4 * x.size * 2),
    )(index, *ins)


def pick_kv_kernel(index_ref, here_ref, *refs):
    own_refs, (o_ref, kv_ref) = refs[:-2], refs[-2:]
    groups = len(own_refs)
    tiles = own_refs[0].shape[0] // TILE
    both = kv_ref.shape[2]
    lanes = own_refs[0].shape[1] - both
    for o, ref in enumerate(own_refs):
        home = lax.rem(here_ref[0] + groups - o, groups) * tiles
        for i in range(tiles):
            kv_ref[home + i] = ref[i * TILE : (i + 1) * TILE, lanes:]

    def step(d, carry):
        o_ref[d] = kv_ref[index_ref[d]]
        return carry

    lax.fori_loop(0, o_ref.shape[0], step, 0)


def pick_kv(index, here, own, dests):
    rows, lanes = own[0].shape
    both = lanes * 2 // 3
    out = (dests, TILE, both)
    return pl.pallas_call(
        pick_kv_kernel,
        grid_spec=pltpu.PrefetchScalarGridSpec(
            num_scalar_prefetch=2,
            grid=(1,),
            in_specs=[pl.BlockSpec((rows, lanes), lambda i, idx, here: (0, 0))] * len(own),
            out_specs=pl.BlockSpec(out, lambda i, idx, here: (0, 0, 0)),
            scratch_shapes=[pltpu.VMEM((len(own) * rows // TILE, TILE, both), jnp.bfloat16)],
        ),
        out_shape=jax.ShapeDtypeStruct(out, jnp.bfloat16),
        cost_estimate=pl.CostEstimate(
            flops=0, transcendentals=0, bytes_accessed=10 * len(own) * rows * lanes // 3
        ),
        name="pick_kv",
    )(index, here, *own)


def split_heads(q):
    first = lax.broadcasted_iota(jnp.int32, q.shape, 1) < HEAD_DIM
    zero = jnp.zeros_like(q)
    return jnp.concatenate([jnp.where(first, q, zero), jnp.where(first, zero, q)], axis=0)


def join_heads(both):
    half = both.shape[0] // 2
    shape = (half, 2 * HEAD_DIM)
    first = lax.broadcasted_iota(jnp.int32, shape, 1) < HEAD_DIM
    return jnp.where(
        first, jnp.broadcast_to(both[:half], shape), jnp.broadcast_to(both[half:], shape)
    )


def score(q2, keys):
    return lax.dot_general(q2, keys, (((1,), (1,)), ((), ())), preferred_element_type=jnp.float32)


def local_kernel(place_ref, *refs, groups):
    own_refs, ext_refs = refs[:groups], refs[groups : 2 * groups]
    m_ref, l_ref, a_ref, qo_ref, q_ref, pad_ref = refs[2 * groups :]
    own_rows = own_refs[0].shape[0]
    part = ext_refs[0].shape[0] // (2 + GLOBALS)
    tiles_here = own_rows * groups // TILE
    lanes = m_ref.shape[1]
    step = pl.program_id(0)
    per_step = m_ref.shape[0] // TILE

    @pl.when(step == 0)
    def _():
        homes = [0] + [tiles_here + 1 + i for i in range(1 + GLOBALS)]
        for o in range(groups):
            row = pl.multiple_of(lax.rem(place_ref[2] + groups - o, groups) * own_rows, own_rows)
            q_ref[pl.ds(row, own_rows), :] = own_refs[o][:, :lanes]
            pad_ref[pl.ds(row + TILE, own_rows), :] = own_refs[o][:, lanes:]
            for i, home in enumerate(homes):
                row = home * TILE + o * part
                pad_ref[row : row + part, :] = ext_refs[o][i * part : (i + 1) * part, :]

    tiles_total = place_ref[1]
    global_kv = pad_ref[(tiles_here + 2) * TILE :, :]
    for i in range(per_step):
        t = step * per_step + i
        rows = pl.ds(i * TILE, TILE)
        q = q_ref[pl.ds(pl.multiple_of(t * TILE, TILE), TILE), :]
        q2 = split_heads(q)
        window = pad_ref[pl.ds(pl.multiple_of(t * TILE, TILE), 3 * TILE), :]
        first_id = place_ref[0] * tiles_here + t - 1
        position = lax.broadcasted_iota(jnp.int32, (2 * TILE, 3 * TILE), 1)
        ok = (position >= (GLOBALS - first_id) * TILE) & (
            position < (tiles_total - first_id) * TILE
        )
        s_window = jnp.where(ok, score(q2, window[:, :lanes]), NEG)
        s_global = score(q2, global_kv[:, :lanes])
        top = jnp.maximum(
            jnp.max(s_window, axis=1, keepdims=True), jnp.max(s_global, axis=1, keepdims=True)
        )
        p_window = jnp.exp2((s_window - top) * SCALE)
        p_global = jnp.exp2((s_global - top) * SCALE)
        total = jnp.sum(p_window, axis=1, keepdims=True) + jnp.sum(p_global, axis=1, keepdims=True)
        acc = jnp.dot(
            p_window.astype(jnp.bfloat16), window[:, lanes:], preferred_element_type=jnp.float32
        ) + jnp.dot(
            p_global.astype(jnp.bfloat16), global_kv[:, lanes:], preferred_element_type=jnp.float32
        )
        m_ref[rows, :] = join_heads(top)
        l_ref[rows, :] = join_heads(total)
        a_ref[rows, :] = join_heads(acc)
        qo_ref[rows, :] = q


def local_attention(place, own, ext, ext_rows, per_step=2):
    groups = len(own)
    rows = own[0].shape[0] * groups
    both = ext[0].shape[1]
    lanes = both // 2
    block = pl.BlockSpec((per_step * TILE, lanes), lambda i, s: (i, 0))
    last = ext[0].shape[0] // ext_rows - 1
    out = jax.ShapeDtypeStruct((rows, lanes), jnp.float32)
    keys = (3 + GLOBALS) * TILE
    return pl.pallas_call(
        functools.partial(local_kernel, groups=groups),
        grid_spec=pltpu.PrefetchScalarGridSpec(
            num_scalar_prefetch=1,
            grid=(rows // (per_step * TILE),),
            in_specs=[pl.BlockSpec(a.shape, lambda i, s: (0, 0)) for a in own]
            + [pl.BlockSpec((ext_rows, both), lambda i, s: (last, 0)) for _ in ext],
            out_specs=[block] * 4,
            scratch_shapes=[
                pltpu.VMEM((rows, lanes), jnp.bfloat16),
                pltpu.VMEM((rows + (2 + GLOBALS) * TILE, both), jnp.bfloat16),
            ],
        ),
        out_shape=[out] * 3 + [jax.ShapeDtypeStruct((rows, lanes), jnp.bfloat16)],
        cost_estimate=pl.CostEstimate(
            flops=8 * rows * keys * lanes,
            transcendentals=2 * rows * keys,
            bytes_accessed=rows * lanes * 20,
        ),
        name="local_attention",
    )(place, *own, *ext)


def random_kernel(index_ref, count_ref, *refs, groups, spread):
    part_refs, whole_refs = refs[: spread * groups], refs[spread * groups : spread * groups + CAP - spread]
    q_ref, m_ref, l_ref, a_ref, o_ref, kv_ref, sems = refs[spread * groups + CAP - spread :]
    lanes = q_ref.shape[1]
    step = pl.program_id(0)
    per_step = q_ref.shape[0] // TILE
    part = TILE // groups
    shards = kv_ref.shape[0] // CAP

    @pl.when(step == 0)
    def _():
        copies = []
        for i, ref in enumerate(part_refs):
            s, o = divmod(i, groups)
            home = kv_ref.at[s * shards : (s + 1) * shards, o * part : (o + 1) * part, :]
            copies.append(pltpu.make_async_copy(ref.at[:shards], home, sems.at[i]))
        for i, ref in enumerate(whole_refs):
            home = kv_ref.at[(spread + i) * shards : (spread + i + 1) * shards]
            copies.append(pltpu.make_async_copy(ref, home, sems.at[spread * groups + i]))
        for copy in copies:
            copy.start()
        for copy in copies:
            copy.wait()

    for i in range(per_step):
        t = step * per_step + i
        rows = pl.ds(i * TILE, TILE)
        q2 = split_heads(q_ref[rows, :])
        count = count_ref[t]
        at = [index_ref[t * RANDOM + j] for j in range(RANDOM)]
        scores = []
        top = None
        for j in range(0, RANDOM, 2):
            keys = jnp.concatenate([kv_ref[at[j], :, :lanes], kv_ref[at[j + 1], :, :lanes]], axis=0)
            s = score(q2, keys)
            for i, part in enumerate((s[:, :TILE], s[:, TILE:])):
                part = part + jnp.where(j + i < count, 0.0, NEG).astype(jnp.float32)
                scores.append(part)
                top = part if top is None else jnp.maximum(top, part)
        m_old = m_ref[rows, :]
        m_old = jnp.concatenate([m_old[:, :1], m_old[:, HEAD_DIM : HEAD_DIM + 1]], axis=0)
        m_new = jnp.maximum(jnp.max(top, axis=1, keepdims=True), m_old)
        alpha = jnp.exp2((m_old - m_new) * SCALE)
        total = None
        acc = None
        for j in range(0, RANDOM, 2):
            p0 = jnp.exp2((scores[j] - m_new) * SCALE)
            p1 = jnp.exp2((scores[j + 1] - m_new) * SCALE)
            total = p0 + p1 if total is None else total + (p0 + p1)
            p = jnp.concatenate([p0.astype(jnp.bfloat16), p1.astype(jnp.bfloat16)], axis=1)
            v = jnp.concatenate([kv_ref[at[j], :, lanes:], kv_ref[at[j + 1], :, lanes:]], axis=0)
            part = jnp.dot(p, v, preferred_element_type=jnp.float32)
            acc = part if acc is None else acc + part
        alpha = join_heads(alpha)
        denominator = l_ref[rows, :] * alpha + join_heads(jnp.sum(total, axis=1, keepdims=True))
        numerator = a_ref[rows, :] * alpha + join_heads(acc)
        o_ref[rows, :] = (numerator / denominator).astype(jnp.bfloat16)


def random_attention(index, count, q, parts, whole, m, l, a, per_step=8):
    rows, lanes = q.shape
    groups = len(parts[0])
    spread = len(parts)
    shards = whole[0].shape[0]
    part = TILE // groups
    flat = [f.reshape(-1, part, 2 * lanes) for slot in parts for f in slot]
    block = pl.BlockSpec((per_step * TILE, lanes), lambda i, s, c: (i, 0))
    keys = RANDOM * TILE
    sources = len(flat) + len(whole)
    return pl.pallas_call(
        functools.partial(random_kernel, groups=groups, spread=spread),
        grid_spec=pltpu.PrefetchScalarGridSpec(
            num_scalar_prefetch=2,
            grid=(rows // (per_step * TILE),),
            in_specs=[pl.BlockSpec(memory_space=pl.ANY)] * sources + [block] * 4,
            out_specs=block,
            scratch_shapes=[
                pltpu.VMEM((CAP * shards, TILE, 2 * lanes), jnp.bfloat16),
                pltpu.SemaphoreType.DMA((sources,)),
            ],
        ),
        out_shape=jax.ShapeDtypeStruct((rows, lanes), jnp.bfloat16),
        cost_estimate=pl.CostEstimate(
            flops=8 * rows * keys * lanes,
            transcendentals=2 * rows * keys,
            bytes_accessed=rows * lanes * 16 + CAP * shards * TILE * lanes * 4,
        ),
        name="random_attention",
    )(index, count, *flat, *whole, q, m, l, a)


def request_tables(random_tiles, random_count, shard, ctx_count, tiles_here):
    slots = random_tiles.shape[1]
    live = jnp.arange(slots, dtype=jnp.int32)[None, :] < random_count[:, None]
    entries = jnp.where(live, random_tiles, -1).reshape(ctx_count, tiles_here * slots)
    mine = shard * tiles_here + jnp.arange(tiles_here, dtype=jnp.int32)
    owned = jnp.any(entries[:, :, None] == mine[None, None, :], axis=1)
    k = jnp.arange(tiles_here, dtype=jnp.int32)
    rank = jnp.sum((owned[:, None, :] & (k[None, None, :] < k[None, :, None])).astype(jnp.int32), axis=2)
    hit = owned[:, None, :] & (rank[:, None, :] == jnp.arange(CAP, dtype=jnp.int32)[None, :, None])
    send = jnp.sum(jnp.where(hit, k[None, None, :], 0), axis=2)
    wanted = lax.dynamic_index_in_dim(entries, shard, 0, keepdims=False)
    tiles = jnp.arange(ctx_count * tiles_here, dtype=jnp.int32)
    needed = jnp.any(wanted[:, None] == tiles[None, :], axis=0)
    owner = wanted // tiles_here
    lower = (
        needed[None, :]
        & (tiles[None, :] < wanted[:, None])
        & (tiles[None, :] >= (owner * tiles_here)[:, None])
    )
    slot = jnp.sum(lower.astype(jnp.int32), axis=1)
    read = jnp.where(wanted >= 0, slot * ctx_count + owner, 0)
    return [send[:, slot] for slot in range(CAP)], read


def body(tokens, w_query, w_key, w_value, w_out, random_tiles, random_count):
    groups = lax.axis_size("head")
    ctx_count = lax.axis_size("ctx")
    rows, width = tokens.shape
    own_tiles = rows // TILE
    part = TILE // groups
    tiles_here = own_tiles * groups
    shard = lax.axis_index("ctx").astype(jnp.int32)

    here = lax.axis_index("head").astype(jnp.int32)

    striped = tokens.reshape(own_tiles, groups, part, width).transpose(1, 0, 2, 3)
    striped = lax.all_to_all(striped, "head", split_axis=0, concat_axis=0, tiled=True)
    striped = striped.reshape(tiles_here, part, width)
    send, read = request_tables(random_tiles, random_count, shard, ctx_count, tiles_here)
    head = here[None]

    own = project(head, [tokens], rows, [w_query, w_key, w_value], groups, place_rows)
    own = exchange(own, "head")

    up = [(i, i + 1) for i in range(ctx_count - 1)]
    down = [(j, i) for i, j in up]
    before = lax.ppermute(striped[-1:], "ctx", up)
    after = lax.ppermute(striped[:1], "ctx", down)
    edges = jnp.concatenate([before, after], axis=0).reshape(2 * part, width)

    fetched, got = [], None
    for slot in range(CAP - 1):
        chunks = pick_chunks(send[slot], striped, ctx_count, got)
        got = lax.all_to_all(chunks, "ctx", split_axis=0, concat_axis=0, tiled=True)
        count = ctx_count * part
        if slot == 0:
            xs, place = [got], place_chunks
        else:
            xs, place, count = [got, edges], place_chunks_and_edges, count + (2 + GLOBALS) * part
        projected = project(head, xs, count, [w_key, w_value], groups, place)
        fetched.append(exchange(projected, "head"))
    chosen = pick_kv(send[CAP - 1], head, own, ctx_count)
    whole = lax.all_to_all(chosen, "ctx", split_axis=0, concat_axis=0, tiled=True)

    where = jnp.stack([shard, jnp.int32(tiles_here * ctx_count), here])
    m, l, a, q = local_attention(where, own, fetched[1], (2 + GLOBALS) * part)
    my_count = lax.dynamic_slice_in_dim(random_count, shard * tiles_here, tiles_here, 0)
    attended = random_attention(read, my_count, q, fetched, [whole], m, l, a)
    attended = attended.reshape(groups, rows, -1)
    returned = lax.all_to_all(attended, "head", split_axis=0, concat_axis=0, tiled=True)
    out = lax.dot_general(
        returned,
        w_out.reshape(groups, -1, width),
        (((0, 2), (0, 1)), ((), ())),
        preferred_element_type=jnp.float32,
    )
    return out.astype(jnp.bfloat16)


def solution(mesh):
    return jax.shard_map(
        body,
        mesh=mesh,
        in_specs=(P(("ctx", "head"), None), P(), P(), P(), P(), P(), P()),
        out_specs=P(("ctx", "head"), None),
        check_vma=False,
    )
```

```python
import functools

import jax
import jax.numpy as jnp
from jax import lax
from jax.experimental import pallas as pl
from jax.experimental.pallas import tpu as pltpu
from jax.sharding import PartitionSpec as P


HEAD_DIM = 64
TILE = 128
GLOBALS = 2
RANDOM = 12
CAP = 3
LOG2E = 1.4426950408889634
SCALE = HEAD_DIM ** (-0.5) * LOG2E
NEG = -1e30
LANES = 128
SUB = 8


def project_kernel(here_ref, *refs, sources, weights, groups, place):
    x_refs, rest = refs[:sources], refs[sources:]
    w_refs, o_refs, x_ref = rest[:weights], rest[weights : weights + groups], rest[-1]
    e_refs = rest[weights + groups : -1]
    step = pl.program_id(0)

    @pl.when(step == 0)
    def _():
        place(x_ref, *x_refs)

    w = jnp.concatenate([ref[...] for ref in w_refs], axis=1)
    r = jnp.dot(x_ref[...], w, preferred_element_type=jnp.float32).astype(jnp.bfloat16)
    for o, o_ref in enumerate(o_refs):

        @pl.when(step == o)
        def _():
            o_ref[...] = r[: o_ref.shape[0]]
            if e_refs:
                e_refs[o][...] = r[o_ref.shape[0] :]


def place_rows(x_ref, rows_ref):
    x_ref[...] = rows_ref[...]


def place_chunks(x_ref, got_ref):
    shards, _, lanes = got_ref.shape
    part = x_ref.shape[0] // shards
    for k in range(x_ref.shape[1] // lanes):
        x_ref[:, k * lanes : (k + 1) * lanes] = got_ref[:, k * part : (k + 1) * part, :].reshape(
            shards * part, lanes
        )


def place_chunks_and_edges(x_ref, got_ref, edge_ref):
    shards, tall, lanes = got_ref.shape
    edges = edge_ref.shape[0]
    width = x_ref.shape[1]
    across = width // lanes
    extra = shards * SUB // across
    rows = x_ref.shape[0] - edges - extra
    place_chunks(x_ref.at[:rows], got_ref)
    x_ref[rows : rows + edges] = edge_ref[...]
    for b in range(shards):
        row = rows + edges + b // across * SUB
        lane = b % across * lanes
        x_ref[row : row + SUB, lane : lane + lanes] = got_ref[b, tall - SUB :, :]


def project(here, xs, rows, ws, groups, place, extra=0):
    width = ws[0].shape[0]
    lanes = ws[0].shape[1] // groups
    out_lanes = lanes * len(ws)
    outs = [(rows, out_lanes)] * groups + [(extra, out_lanes)] * (groups if extra else 0)
    rows = rows + extra
    return pl.pallas_call(
        functools.partial(
            project_kernel, sources=len(xs), weights=len(ws), groups=groups, place=place
        ),
        grid_spec=pltpu.PrefetchScalarGridSpec(
            num_scalar_prefetch=1,
            grid=(groups,),
            in_specs=[
                pl.BlockSpec(x.shape, lambda o, here, n=len(x.shape): (0,) * n) for x in xs
            ]
            + [
                pl.BlockSpec((width, lanes), lambda o, here: (0, lax.rem(here[0] + o, groups)))
                for _ in ws
            ],
            out_specs=[pl.BlockSpec(out, lambda o, here: (0, 0)) for out in outs],
            scratch_shapes=[pltpu.VMEM((rows, width), jnp.bfloat16)],
        ),
        out_shape=[jax.ShapeDtypeStruct(out, jnp.bfloat16) for out in outs],
        cost_estimate=pl.CostEstimate(
            flops=2 * rows * width * lanes * len(ws) * groups,
            transcendentals=0,
            bytes_accessed=2 * width * lanes * len(ws) * groups + 2 * rows * (width + out_lanes * groups),
        ),
    )(here, *xs, *ws)


def exchange(pieces, axis):
    size = len(pieces)
    return [pieces[0]] + [
        lax.ppermute(pieces[o], axis, [(i, (i + o) % size) for i in range(size)])
        for o in range(1, size)
    ]


def pick_chunk(o_ref, d, tile):
    lanes = o_ref.shape[2]
    part, width = tile.shape
    for k in range(width // lanes):
        o_ref[d, k * part : (k + 1) * part, :] = tile[:, k * lanes : (k + 1) * lanes]


def pick_first_kernel(index_ref, x_ref, o_ref):
    dests, tall, lanes = o_ref.shape
    part, width = x_ref.shape[1:]
    across = width // lanes

    def step(d, carry):
        pick_chunk(o_ref, d, x_ref[index_ref[d]])
        return carry

    lax.fori_loop(0, dests, step, 0)
    for b in range(dests):
        row = b // across * SUB
        lane = b % across * lanes
        o_ref[b, tall - SUB :, :] = x_ref[
            row // part, row % part : row % part + SUB, lane : lane + lanes
        ]


def pick_second_kernel(index_ref, x_ref, root_ref, o_ref):
    dests, tall, _ = o_ref.shape
    block = root_ref[0]

    def step(d, carry):
        pick_chunk(o_ref, d, x_ref[index_ref[d]])
        o_ref[d, tall - SUB :, :] = block
        return carry

    lax.fori_loop(0, dests, step, 0)


def pick_chunks(index, x, dests, got):
    _, part, width = x.shape
    tall = part * width // LANES + SUB
    out = (dests, tall, LANES)
    whole = lambda shape: pl.BlockSpec(shape, lambda i, idx: (0,) * len(shape))
    ins, specs, kernel = [x], [whole(x.shape)], pick_first_kernel
    if got is not None:
        ins.append(got)
        specs.append(pl.BlockSpec((1, SUB, LANES), lambda i, idx: (0, tall // SUB - 1, 0)))
        kernel = pick_second_kernel
    return pl.pallas_call(
        kernel,
        grid_spec=pltpu.PrefetchScalarGridSpec(
            num_scalar_prefetch=1, grid=(1,), in_specs=specs, out_specs=whole(out)
        ),
        out_shape=jax.ShapeDtypeStruct(out, x.dtype),
        cost_estimate=pl.CostEstimate(flops=0, transcendentals=0, bytes_accessed=4 * x.size * 2),
    )(index, *ins)


def pick_kv_kernel(index_ref, here_ref, *refs):
    own_refs, (o_ref, kv_ref) = refs[:-2], refs[-2:]
    groups = len(own_refs)
    tiles = own_refs[0].shape[0] // TILE
    both = kv_ref.shape[2]
    lanes = own_refs[0].shape[1] - both
    for o, ref in enumerate(own_refs):
        home = lax.rem(here_ref[0] + groups - o, groups) * tiles
        for i in range(tiles):
            kv_ref[home + i] = ref[i * TILE : (i + 1) * TILE, lanes:]

    def step(d, carry):
        o_ref[d] = kv_ref[index_ref[d]]
        return carry

    lax.fori_loop(0, o_ref.shape[0], step, 0)


def pick_kv(index, here, own, dests):
    rows, lanes = own[0].shape
    both = lanes * 2 // 3
    out = (dests, TILE, both)
    return pl.pallas_call(
        pick_kv_kernel,
        grid_spec=pltpu.PrefetchScalarGridSpec(
            num_scalar_prefetch=2,
            grid=(1,),
            in_specs=[pl.BlockSpec((rows, lanes), lambda i, idx, here: (0, 0))] * len(own),
            out_specs=pl.BlockSpec(out, lambda i, idx, here: (0, 0, 0)),
            scratch_shapes=[pltpu.VMEM((len(own) * rows // TILE, TILE, both), jnp.bfloat16)],
        ),
        out_shape=jax.ShapeDtypeStruct(out, jnp.bfloat16),
        cost_estimate=pl.CostEstimate(
            flops=0, transcendentals=0, bytes_accessed=10 * len(own) * rows * lanes // 3
        ),
        name="pick_kv",
    )(index, here, *own)


def split_heads(q):
    first = lax.broadcasted_iota(jnp.int32, q.shape, 1) < HEAD_DIM
    zero = jnp.zeros_like(q)
    return jnp.concatenate([jnp.where(first, q, zero), jnp.where(first, zero, q)], axis=0)


def join_heads(both):
    half = both.shape[0] // 2
    shape = (half, 2 * HEAD_DIM)
    first = lax.broadcasted_iota(jnp.int32, shape, 1) < HEAD_DIM
    return jnp.where(
        first, jnp.broadcast_to(both[:half], shape), jnp.broadcast_to(both[half:], shape)
    )


def score(q2, keys):
    return lax.dot_general(q2, keys, (((1,), (1,)), ((), ())), preferred_element_type=jnp.float32)


def local_kernel(place_ref, *refs, groups):
    own_refs, ext_refs = refs[:groups], refs[groups : 2 * groups]
    m_ref, l_ref, a_ref, qo_ref, q_ref, pad_ref = refs[2 * groups :]
    own_rows = own_refs[0].shape[0]
    part = ext_refs[0].shape[0] // (2 + GLOBALS)
    tiles_here = own_rows * groups // TILE
    lanes = m_ref.shape[1]
    step = pl.program_id(0)
    per_step = m_ref.shape[0] // TILE

    @pl.when(step == 0)
    def _():
        homes = [0] + [tiles_here + 1 + i for i in range(1 + GLOBALS)]
        for o in range(groups):
            row = pl.multiple_of(lax.rem(place_ref[2] + groups - o, groups) * own_rows, own_rows)
            q_ref[pl.ds(row, own_rows), :] = own_refs[o][:, :lanes]
            pad_ref[pl.ds(row + TILE, own_rows), :] = own_refs[o][:, lanes:]
            for i, home in enumerate(homes):
                row = home * TILE + o * part
                pad_ref[row : row + part, :] = ext_refs[o][i * part : (i + 1) * part, :]

    tiles_total = place_ref[1]
    global_kv = pad_ref[(tiles_here + 2) * TILE :, :]
    for i in range(per_step):
        t = step * per_step + i
        rows = pl.ds(i * TILE, TILE)
        q = q_ref[pl.ds(pl.multiple_of(t * TILE, TILE), TILE), :]
        q2 = split_heads(q)
        window = pad_ref[pl.ds(pl.multiple_of(t * TILE, TILE), 3 * TILE), :]
        first_id = place_ref[0] * tiles_here + t - 1
        position = lax.broadcasted_iota(jnp.int32, (2 * TILE, 3 * TILE), 1)
        ok = (position >= (GLOBALS - first_id) * TILE) & (
            position < (tiles_total - first_id) * TILE
        )
        s_window = jnp.where(ok, score(q2, window[:, :lanes]), NEG)
        s_global = score(q2, global_kv[:, :lanes])
        top = jnp.maximum(
            jnp.max(s_window, axis=1, keepdims=True), jnp.max(s_global, axis=1, keepdims=True)
        )
        p_window = jnp.exp2((s_window - top) * SCALE)
        p_global = jnp.exp2((s_global - top) * SCALE)
        total = jnp.sum(p_window, axis=1, keepdims=True) + jnp.sum(p_global, axis=1, keepdims=True)
        acc = jnp.dot(
            p_window.astype(jnp.bfloat16), window[:, lanes:], preferred_element_type=jnp.float32
        ) + jnp.dot(
            p_global.astype(jnp.bfloat16), global_kv[:, lanes:], preferred_element_type=jnp.float32
        )
        m_ref[rows, :] = join_heads(top)
        l_ref[rows, :] = join_heads(total)
        a_ref[rows, :] = join_heads(acc)
        qo_ref[rows, :] = q


def local_attention(place, own, ext, per_step=4):
    groups = len(own)
    rows = own[0].shape[0] * groups
    both = ext[0].shape[1]
    lanes = both // 2
    block = pl.BlockSpec((per_step * TILE, lanes), lambda i, s: (i, 0))
    out = jax.ShapeDtypeStruct((rows, lanes), jnp.float32)
    keys = (3 + GLOBALS) * TILE
    return pl.pallas_call(
        functools.partial(local_kernel, groups=groups),
        grid_spec=pltpu.PrefetchScalarGridSpec(
            num_scalar_prefetch=1,
            grid=(rows // (per_step * TILE),),
            in_specs=[pl.BlockSpec(a.shape, lambda i, s: (0, 0)) for a in own]
            + [pl.BlockSpec(a.shape, lambda i, s: (0, 0)) for a in ext],
            out_specs=[block] * 4,
            scratch_shapes=[
                pltpu.VMEM((rows, lanes), jnp.bfloat16),
                pltpu.VMEM((rows + (2 + GLOBALS) * TILE, both), jnp.bfloat16),
            ],
        ),
        out_shape=[out] * 3 + [jax.ShapeDtypeStruct((rows, lanes), jnp.bfloat16)],
        cost_estimate=pl.CostEstimate(
            flops=8 * rows * keys * lanes,
            transcendentals=2 * rows * keys,
            bytes_accessed=rows * lanes * 20,
        ),
        name="local_attention",
    )(place, *own, *ext)


def random_kernel(index_ref, count_ref, *refs, groups, spread):
    part_refs, whole_refs = refs[: spread * groups], refs[spread * groups : spread * groups + CAP - spread]
    q_ref, m_ref, l_ref, a_ref, o_ref, kv_ref, sems = refs[spread * groups + CAP - spread :]
    lanes = q_ref.shape[1]
    step = pl.program_id(0)
    per_step = q_ref.shape[0] // TILE
    part = TILE // groups
    shards = kv_ref.shape[0] // CAP

    @pl.when(step == 0)
    def _():
        copies = []
        for i, ref in enumerate(part_refs):
            s, o = divmod(i, groups)
            home = kv_ref.at[s * shards : (s + 1) * shards, o * part : (o + 1) * part, :]
            copies.append(pltpu.make_async_copy(ref.at[:shards], home, sems.at[i]))
        for i, ref in enumerate(whole_refs):
            home = kv_ref.at[(spread + i) * shards : (spread + i + 1) * shards]
            copies.append(pltpu.make_async_copy(ref, home, sems.at[spread * groups + i]))
        for copy in copies:
            copy.start()
        for copy in copies:
            copy.wait()

    for i in range(per_step):
        t = step * per_step + i
        rows = pl.ds(i * TILE, TILE)
        q2 = split_heads(q_ref[rows, :])
        count = count_ref[t]
        at = [index_ref[t * RANDOM + j] for j in range(RANDOM)]
        scores = []
        top = None
        for j in range(0, RANDOM, 2):
            keys = jnp.concatenate([kv_ref[at[j], :, :lanes], kv_ref[at[j + 1], :, :lanes]], axis=0)
            s = score(q2, keys)
            for i, part in enumerate((s[:, :TILE], s[:, TILE:])):
                part = part + jnp.where(j + i < count, 0.0, NEG).astype(jnp.float32)
                scores.append(part)
                top = part if top is None else jnp.maximum(top, part)
        m_old = m_ref[rows, :]
        m_old = jnp.concatenate([m_old[:, :1], m_old[:, HEAD_DIM : HEAD_DIM + 1]], axis=0)
        m_new = jnp.maximum(jnp.max(top, axis=1, keepdims=True), m_old)
        alpha = jnp.exp2((m_old - m_new) * SCALE)
        total = None
        acc = None
        for j in range(0, RANDOM, 2):
            p0 = jnp.exp2((scores[j] - m_new) * SCALE)
            p1 = jnp.exp2((scores[j + 1] - m_new) * SCALE)
            total = p0 + p1 if total is None else total + (p0 + p1)
            p = jnp.concatenate([p0.astype(jnp.bfloat16), p1.astype(jnp.bfloat16)], axis=1)
            v = jnp.concatenate([kv_ref[at[j], :, lanes:], kv_ref[at[j + 1], :, lanes:]], axis=0)
            part = jnp.dot(p, v, preferred_element_type=jnp.float32)
            acc = part if acc is None else acc + part
        alpha = join_heads(alpha)
        denominator = l_ref[rows, :] * alpha + join_heads(jnp.sum(total, axis=1, keepdims=True))
        numerator = a_ref[rows, :] * alpha + join_heads(acc)
        o_ref[rows, :] = (numerator / denominator).astype(jnp.bfloat16)


def random_attention(index, count, q, parts, whole, m, l, a, per_step=8):
    rows, lanes = q.shape
    groups = len(parts[0])
    spread = len(parts)
    shards = whole[0].shape[0]
    part = TILE // groups
    flat = [f.reshape(-1, part, 2 * lanes) for slot in parts for f in slot]
    block = pl.BlockSpec((per_step * TILE, lanes), lambda i, s, c: (i, 0))
    keys = RANDOM * TILE
    sources = len(flat) + len(whole)
    return pl.pallas_call(
        functools.partial(random_kernel, groups=groups, spread=spread),
        grid_spec=pltpu.PrefetchScalarGridSpec(
            num_scalar_prefetch=2,
            grid=(rows // (per_step * TILE),),
            in_specs=[pl.BlockSpec(memory_space=pl.ANY)] * sources + [block] * 4,
            out_specs=block,
            scratch_shapes=[
                pltpu.VMEM((CAP * shards, TILE, 2 * lanes), jnp.bfloat16),
                pltpu.SemaphoreType.DMA((sources,)),
            ],
        ),
        out_shape=jax.ShapeDtypeStruct((rows, lanes), jnp.bfloat16),
        cost_estimate=pl.CostEstimate(
            flops=8 * rows * keys * lanes,
            transcendentals=2 * rows * keys,
            bytes_accessed=rows * lanes * 16 + CAP * shards * TILE * lanes * 4,
        ),
        name="random_attention",
    )(index, count, *flat, *whole, q, m, l, a)


def request_tables(random_tiles, random_count, shard, ctx_count, tiles_here):
    slots = random_tiles.shape[1]
    live = jnp.arange(slots, dtype=jnp.int32)[None, :] < random_count[:, None]
    entries = jnp.where(live, random_tiles, -1).reshape(ctx_count, tiles_here * slots)
    mine = shard * tiles_here + jnp.arange(tiles_here, dtype=jnp.int32)
    owned = jnp.any(entries[:, :, None] == mine[None, None, :], axis=1)
    k = jnp.arange(tiles_here, dtype=jnp.int32)
    rank = jnp.sum((owned[:, None, :] & (k[None, None, :] < k[None, :, None])).astype(jnp.int32), axis=2)
    hit = owned[:, None, :] & (rank[:, None, :] == jnp.arange(CAP, dtype=jnp.int32)[None, :, None])
    send = jnp.sum(jnp.where(hit, k[None, None, :], 0), axis=2)
    wanted = lax.dynamic_index_in_dim(entries, shard, 0, keepdims=False)
    tiles = jnp.arange(ctx_count * tiles_here, dtype=jnp.int32)
    needed = jnp.any(wanted[:, None] == tiles[None, :], axis=0)
    owner = wanted // tiles_here
    lower = (
        needed[None, :]
        & (tiles[None, :] < wanted[:, None])
        & (tiles[None, :] >= (owner * tiles_here)[:, None])
    )
    slot = jnp.sum(lower.astype(jnp.int32), axis=1)
    read = jnp.where(wanted >= 0, slot * ctx_count + owner, 0)
    return [send[:, slot] for slot in range(CAP)], read


def body(tokens, w_query, w_key, w_value, w_out, random_tiles, random_count):
    groups = lax.axis_size("head")
    ctx_count = lax.axis_size("ctx")
    rows, width = tokens.shape
    own_tiles = rows // TILE
    part = TILE // groups
    tiles_here = own_tiles * groups
    shard = lax.axis_index("ctx").astype(jnp.int32)

    here = lax.axis_index("head").astype(jnp.int32)

    striped = tokens.reshape(own_tiles, groups, part, width).transpose(1, 0, 2, 3)
    striped = lax.all_to_all(striped, "head", split_axis=0, concat_axis=0, tiled=True)
    striped = striped.reshape(tiles_here, part, width)
    send, read = request_tables(random_tiles, random_count, shard, ctx_count, tiles_here)
    head = here[None]

    own = project(head, [tokens], rows, [w_query, w_key, w_value], groups, place_rows)
    own = exchange(own, "head")

    up = [(i, i + 1) for i in range(ctx_count - 1)]
    down = [(j, i) for i, j in up]
    before = lax.ppermute(striped[-1:], "ctx", up)
    after = lax.ppermute(striped[:1], "ctx", down)
    edges = jnp.concatenate([before, after], axis=0).reshape(2 * part, width)

    fetched, got = [], None
    for slot in range(CAP - 1):
        chunks = pick_chunks(send[slot], striped, ctx_count, got)
        got = lax.all_to_all(chunks, "ctx", split_axis=0, concat_axis=0, tiled=True)
        count = ctx_count * part
        if slot == 0:
            xs, place, extra = [got], place_chunks, 0
        else:
            xs, place, extra = [got, edges], place_chunks_and_edges, (2 + GLOBALS) * part
        projected = project(head, xs, count, [w_key, w_value], groups, place, extra)
        if extra:
            ends = exchange(projected[groups:], "head")
        fetched.append(exchange(projected[:groups], "head"))
    chosen = pick_kv(send[CAP - 1], head, own, ctx_count)
    whole = lax.all_to_all(chosen, "ctx", split_axis=0, concat_axis=0, tiled=True)

    where = jnp.stack([shard, jnp.int32(tiles_here * ctx_count), here])
    m, l, a, q = local_attention(where, own, ends)
    my_count = lax.dynamic_slice_in_dim(random_count, shard * tiles_here, tiles_here, 0)
    attended = random_attention(read, my_count, q, fetched, [whole], m, l, a)
    attended = attended.reshape(groups, rows, -1)
    returned = lax.all_to_all(attended, "head", split_axis=0, concat_axis=0, tiled=True)
    out = lax.dot_general(
        returned,
        w_out.reshape(groups, -1, width),
        (((0, 2), (0, 1)), ((), ())),
        preferred_element_type=jnp.float32,
    )
    return out.astype(jnp.bfloat16)


def solution(mesh):
    return jax.shard_map(
        body,
        mesh=mesh,
        in_specs=(P(("ctx", "head"), None), P(), P(), P(), P(), P(), P()),
        out_specs=P(("ctx", "head"), None),
        check_vma=False,
    )
```

```python
import functools

import jax
import jax.numpy as jnp
from jax import lax
from jax.experimental import pallas as pl
from jax.experimental.pallas import tpu as pltpu
from jax.sharding import PartitionSpec as P


HEAD_DIM = 64
TILE = 128
GLOBALS = 2
RANDOM = 12
CAP = 3
LOG2E = 1.4426950408889634
SCALE = HEAD_DIM ** (-0.5) * LOG2E
NEG = -1e30
LANES = 128
SUB = 8


def project_kernel(here_ref, *refs, sources, weights, groups, place):
    x_refs, rest = refs[:sources], refs[sources:]
    w_refs, o_refs, x_ref = rest[:weights], rest[weights : weights + groups], rest[-1]
    e_refs = rest[weights + groups : -1]
    step = pl.program_id(0)

    @pl.when(step == 0)
    def _():
        place(x_ref, *x_refs)

    w = jnp.concatenate([ref[...] for ref in w_refs], axis=1)
    r = jnp.dot(x_ref[...], w, preferred_element_type=jnp.float32).astype(jnp.bfloat16)
    for o, o_ref in enumerate(o_refs):

        @pl.when(step == o)
        def _():
            o_ref[...] = r[: o_ref.shape[0]]
            if e_refs:
                e_refs[o][...] = r[o_ref.shape[0] :]


def place_rows(x_ref, rows_ref):
    x_ref[...] = rows_ref[...]


def place_chunks(x_ref, got_ref):
    shards, _, lanes = got_ref.shape
    part = x_ref.shape[0] // shards
    for k in range(x_ref.shape[1] // lanes):
        x_ref[:, k * lanes : (k + 1) * lanes] = got_ref[:, k * part : (k + 1) * part, :].reshape(
            shards * part, lanes
        )


def place_chunks_and_edges(x_ref, got_ref, edge_ref):
    shards, tall, lanes = got_ref.shape
    edges = edge_ref.shape[0]
    width = x_ref.shape[1]
    across = width // lanes
    extra = shards * SUB // across
    rows = x_ref.shape[0] - edges - extra
    place_chunks(x_ref.at[:rows], got_ref)
    x_ref[rows : rows + edges] = edge_ref[...]
    for b in range(shards):
        row = rows + edges + b // across * SUB
        lane = b % across * lanes
        x_ref[row : row + SUB, lane : lane + lanes] = got_ref[b, tall - SUB :, :]


def project(here, xs, rows, ws, groups, place, extra=0):
    width = ws[0].shape[0]
    lanes = ws[0].shape[1] // groups
    out_lanes = lanes * len(ws)
    outs = [(rows, out_lanes)] * groups + [(extra, out_lanes)] * (groups if extra else 0)
    rows = rows + extra
    return pl.pallas_call(
        functools.partial(
            project_kernel, sources=len(xs), weights=len(ws), groups=groups, place=place
        ),
        grid_spec=pltpu.PrefetchScalarGridSpec(
            num_scalar_prefetch=1,
            grid=(groups,),
            in_specs=[
                pl.BlockSpec(x.shape, lambda o, here, n=len(x.shape): (0,) * n) for x in xs
            ]
            + [
                pl.BlockSpec((width, lanes), lambda o, here: (0, lax.rem(here[0] + o, groups)))
                for _ in ws
            ],
            out_specs=[pl.BlockSpec(out, lambda o, here: (0, 0)) for out in outs],
            scratch_shapes=[pltpu.VMEM((rows, width), jnp.bfloat16)],
        ),
        out_shape=[jax.ShapeDtypeStruct(out, jnp.bfloat16) for out in outs],
        cost_estimate=pl.CostEstimate(
            flops=2 * rows * width * lanes * len(ws) * groups,
            transcendentals=0,
            bytes_accessed=2 * width * lanes * len(ws) * groups + 2 * rows * (width + out_lanes * groups),
        ),
    )(here, *xs, *ws)


def exchange(pieces, axis):
    size = len(pieces)
    return [pieces[0]] + [
        lax.ppermute(pieces[o], axis, [(i, (i + o) % size) for i in range(size)])
        for o in range(1, size)
    ]


def pick_chunk(o_ref, d, tile):
    lanes = o_ref.shape[2]
    part, width = tile.shape
    for k in range(width // lanes):
        o_ref[d, k * part : (k + 1) * part, :] = tile[:, k * lanes : (k + 1) * lanes]


def pick_first_kernel(index_ref, x_ref, o_ref):
    dests, tall, lanes = o_ref.shape
    part, width = x_ref.shape[1:]
    across = width // lanes

    def step(d, carry):
        pick_chunk(o_ref, d, x_ref[index_ref[d]])
        return carry

    lax.fori_loop(0, dests, step, 0)
    for b in range(dests):
        row = b // across * SUB
        lane = b % across * lanes
        o_ref[b, tall - SUB :, :] = x_ref[
            row // part, row % part : row % part + SUB, lane : lane + lanes
        ]


def pick_second_kernel(index_ref, x_ref, root_ref, o_ref):
    dests, tall, _ = o_ref.shape
    block = root_ref[0]

    def step(d, carry):
        pick_chunk(o_ref, d, x_ref[index_ref[d]])
        o_ref[d, tall - SUB :, :] = block
        return carry

    lax.fori_loop(0, dests, step, 0)


def pick_chunks(index, x, dests, got):
    _, part, width = x.shape
    tall = part * width // LANES + SUB
    out = (dests, tall, LANES)
    whole = lambda shape: pl.BlockSpec(shape, lambda i, idx: (0,) * len(shape))
    ins, specs, kernel = [x], [whole(x.shape)], pick_first_kernel
    if got is not None:
        ins.append(got)
        specs.append(pl.BlockSpec((1, SUB, LANES), lambda i, idx: (0, tall // SUB - 1, 0)))
        kernel = pick_second_kernel
    return pl.pallas_call(
        kernel,
        grid_spec=pltpu.PrefetchScalarGridSpec(
            num_scalar_prefetch=1, grid=(1,), in_specs=specs, out_specs=whole(out)
        ),
        out_shape=jax.ShapeDtypeStruct(out, x.dtype),
        cost_estimate=pl.CostEstimate(flops=0, transcendentals=0, bytes_accessed=4 * x.size * 2),
    )(index, *ins)


def pick_kv_kernel(index_ref, here_ref, *refs):
    own_refs, (o_ref, kv_ref) = refs[:-2], refs[-2:]
    groups = len(own_refs)
    tiles = own_refs[0].shape[0] // TILE
    both = kv_ref.shape[2]
    lanes = own_refs[0].shape[1] - both
    for o, ref in enumerate(own_refs):
        home = lax.rem(here_ref[0] + groups - o, groups) * tiles
        for i in range(tiles):
            kv_ref[home + i] = ref[i * TILE : (i + 1) * TILE, lanes:]

    def step(d, carry):
        o_ref[d] = kv_ref[index_ref[d]]
        return carry

    lax.fori_loop(0, o_ref.shape[0], step, 0)


def pick_kv(index, here, own, dests):
    rows, lanes = own[0].shape
    both = lanes * 2 // 3
    out = (dests, TILE, both)
    return pl.pallas_call(
        pick_kv_kernel,
        grid_spec=pltpu.PrefetchScalarGridSpec(
            num_scalar_prefetch=2,
            grid=(1,),
            in_specs=[pl.BlockSpec((rows, lanes), lambda i, idx, here: (0, 0))] * len(own),
            out_specs=pl.BlockSpec(out, lambda i, idx, here: (0, 0, 0)),
            scratch_shapes=[pltpu.VMEM((len(own) * rows // TILE, TILE, both), jnp.bfloat16)],
        ),
        out_shape=jax.ShapeDtypeStruct(out, jnp.bfloat16),
        cost_estimate=pl.CostEstimate(
            flops=0, transcendentals=0, bytes_accessed=10 * len(own) * rows * lanes // 3
        ),
        name="pick_kv",
    )(index, here, *own)


def split_heads(q):
    first = lax.broadcasted_iota(jnp.int32, q.shape, 1) < HEAD_DIM
    zero = jnp.zeros_like(q)
    return jnp.concatenate([jnp.where(first, q, zero), jnp.where(first, zero, q)], axis=0)


def join_heads(both):
    half = both.shape[0] // 2
    shape = (half, 2 * HEAD_DIM)
    first = lax.broadcasted_iota(jnp.int32, shape, 1) < HEAD_DIM
    return jnp.where(
        first, jnp.broadcast_to(both[:half], shape), jnp.broadcast_to(both[half:], shape)
    )


def score(q2, keys):
    return lax.dot_general(q2, keys, (((1,), (1,)), ((), ())), preferred_element_type=jnp.float32)


def local_kernel(place_ref, *refs, groups):
    own_refs, ext_refs = refs[:groups], refs[groups : 2 * groups]
    m_ref, l_ref, a_ref, qo_ref, q_ref, pad_ref = refs[2 * groups :]
    own_rows = own_refs[0].shape[0]
    part = ext_refs[0].shape[0] // (2 + GLOBALS)
    tiles_here = own_rows * groups // TILE
    lanes = m_ref.shape[1]
    step = pl.program_id(0)
    per_step = m_ref.shape[0] // TILE

    @pl.when(step == 0)
    def _():
        homes = [0] + [tiles_here + 1 + i for i in range(1 + GLOBALS)]
        for o in range(groups):
            row = pl.multiple_of(lax.rem(place_ref[2] + groups - o, groups) * own_rows, own_rows)
            q_ref[pl.ds(row, own_rows), :] = own_refs[o][:, :lanes]
            pad_ref[pl.ds(row + TILE, own_rows), :] = own_refs[o][:, lanes:]
            for i, home in enumerate(homes):
                row = home * TILE + o * part
                pad_ref[row : row + part, :] = ext_refs[o][i * part : (i + 1) * part, :]

    tiles_total = place_ref[1]
    global_kv = pad_ref[(tiles_here + 2) * TILE :, :]
    ones = jnp.ones((3 * TILE, lanes), jnp.bfloat16)
    for i in range(per_step):
        t = step * per_step + i
        rows = pl.ds(i * TILE, TILE)
        q = q_ref[pl.ds(pl.multiple_of(t * TILE, TILE), TILE), :]
        q2 = split_heads(q)
        window = pad_ref[pl.ds(pl.multiple_of(t * TILE, TILE), 3 * TILE), :]
        first_id = place_ref[0] * tiles_here + t - 1
        position = lax.broadcasted_iota(jnp.int32, (2 * TILE, 3 * TILE), 1)
        ok = (position >= (GLOBALS - first_id) * TILE) & (
            position < (tiles_total - first_id) * TILE
        )
        s_window = jnp.where(ok, score(q2, window[:, :lanes]), NEG)
        s_global = score(q2, global_kv[:, :lanes])
        top = jnp.maximum(
            jnp.max(s_window, axis=1, keepdims=True), jnp.max(s_global, axis=1, keepdims=True)
        )
        p_window = jnp.exp2((s_window - top) * SCALE)
        p_global = jnp.exp2((s_global - top) * SCALE)
        acc = jnp.dot(
            p_window.astype(jnp.bfloat16),
            jnp.concatenate([window[:, lanes:], ones[: 3 * TILE]], axis=1),
            preferred_element_type=jnp.float32,
        ) + jnp.dot(
            p_global.astype(jnp.bfloat16),
            jnp.concatenate([global_kv[:, lanes:], ones[: GLOBALS * TILE]], axis=1),
            preferred_element_type=jnp.float32,
        )
        m_ref[rows, :] = join_heads(top)
        l_ref[rows, :] = join_heads(acc[:, lanes:])
        a_ref[rows, :] = join_heads(acc[:, :lanes])
        qo_ref[rows, :] = q


def local_attention(place, own, ext, per_step=4):
    groups = len(own)
    rows = own[0].shape[0] * groups
    both = ext[0].shape[1]
    lanes = both // 2
    block = pl.BlockSpec((per_step * TILE, lanes), lambda i, s: (i, 0))
    out = jax.ShapeDtypeStruct((rows, lanes), jnp.float32)
    keys = (3 + GLOBALS) * TILE
    return pl.pallas_call(
        functools.partial(local_kernel, groups=groups),
        grid_spec=pltpu.PrefetchScalarGridSpec(
            num_scalar_prefetch=1,
            grid=(rows // (per_step * TILE),),
            in_specs=[pl.BlockSpec(a.shape, lambda i, s: (0, 0)) for a in own]
            + [pl.BlockSpec(a.shape, lambda i, s: (0, 0)) for a in ext],
            out_specs=[block] * 4,
            scratch_shapes=[
                pltpu.VMEM((rows, lanes), jnp.bfloat16),
                pltpu.VMEM((rows + (2 + GLOBALS) * TILE, both), jnp.bfloat16),
            ],
        ),
        out_shape=[out] * 3 + [jax.ShapeDtypeStruct((rows, lanes), jnp.bfloat16)],
        cost_estimate=pl.CostEstimate(
            flops=8 * rows * keys * lanes,
            transcendentals=2 * rows * keys,
            bytes_accessed=rows * lanes * 20,
        ),
        name="local_attention",
    )(place, *own, *ext)


def random_kernel(index_ref, count_ref, *refs, groups, spread):
    part_refs, whole_refs = refs[: spread * groups], refs[spread * groups : spread * groups + CAP - spread]
    q_ref, m_ref, l_ref, a_ref, o_ref, kv_ref, sems = refs[spread * groups + CAP - spread :]
    lanes = q_ref.shape[1]
    step = pl.program_id(0)
    per_step = q_ref.shape[0] // TILE
    part = TILE // groups
    shards = kv_ref.shape[0] // CAP

    @pl.when(step == 0)
    def _():
        copies = []
        for i, ref in enumerate(part_refs):
            s, o = divmod(i, groups)
            home = kv_ref.at[s * shards : (s + 1) * shards, o * part : (o + 1) * part, :]
            copies.append(pltpu.make_async_copy(ref.at[:shards], home, sems.at[i]))
        for i, ref in enumerate(whole_refs):
            home = kv_ref.at[(spread + i) * shards : (spread + i + 1) * shards]
            copies.append(pltpu.make_async_copy(ref, home, sems.at[spread * groups + i]))
        for copy in copies:
            copy.start()
        for copy in copies:
            copy.wait()

    for i in range(per_step):
        t = step * per_step + i
        rows = pl.ds(i * TILE, TILE)
        q2 = split_heads(q_ref[rows, :])
        count = count_ref[t]
        at = [index_ref[t * RANDOM + j] for j in range(RANDOM)]
        scores = []
        top = None
        for j in range(0, RANDOM, 2):
            keys = jnp.concatenate([kv_ref[at[j], :, :lanes], kv_ref[at[j + 1], :, :lanes]], axis=0)
            s = score(q2, keys)
            scores.append(s)
            top = s if top is None else jnp.maximum(top, s)
        m_old = m_ref[rows, :]
        m_old = jnp.concatenate([m_old[:, :1], m_old[:, HEAD_DIM : HEAD_DIM + 1]], axis=0)
        m_new = jnp.maximum(jnp.max(top, axis=1, keepdims=True), m_old)
        alpha = jnp.exp2((m_old - m_new) * SCALE)
        acc = None
        for j in range(0, RANDOM, 2):
            p = jnp.exp2((scores[j // 2] - m_new) * SCALE).astype(jnp.bfloat16)
            v = []
            for i in range(j, j + 2):
                live = jnp.where(i < count, 1.0, 0.0).astype(jnp.float32)
                one = jnp.full((TILE, lanes), live, jnp.float32).astype(jnp.bfloat16)
                v.append(jnp.concatenate([kv_ref[at[i], :, lanes:] * one, one], axis=1))
            part = jnp.dot(p, jnp.concatenate(v, axis=0), preferred_element_type=jnp.float32)
            acc = part if acc is None else acc + part
        total = acc[:, lanes:]
        acc = acc[:, :lanes]
        alpha = join_heads(alpha)
        denominator = l_ref[rows, :] * alpha + join_heads(total)
        numerator = a_ref[rows, :] * alpha + join_heads(acc)
        o_ref[rows, :] = (numerator / denominator).astype(jnp.bfloat16)


def random_attention(index, count, q, parts, whole, m, l, a, per_step=8):
    rows, lanes = q.shape
    groups = len(parts[0])
    spread = len(parts)
    shards = whole[0].shape[0]
    part = TILE // groups
    flat = [f.reshape(-1, part, 2 * lanes) for slot in parts for f in slot]
    block = pl.BlockSpec((per_step * TILE, lanes), lambda i, s, c: (i, 0))
    keys = RANDOM * TILE
    sources = len(flat) + len(whole)
    return pl.pallas_call(
        functools.partial(random_kernel, groups=groups, spread=spread),
        grid_spec=pltpu.PrefetchScalarGridSpec(
            num_scalar_prefetch=2,
            grid=(rows // (per_step * TILE),),
            in_specs=[pl.BlockSpec(memory_space=pl.ANY)] * sources + [block] * 4,
            out_specs=block,
            scratch_shapes=[
                pltpu.VMEM((CAP * shards, TILE, 2 * lanes), jnp.bfloat16),
                pltpu.SemaphoreType.DMA((sources,)),
            ],
        ),
        out_shape=jax.ShapeDtypeStruct((rows, lanes), jnp.bfloat16),
        cost_estimate=pl.CostEstimate(
            flops=8 * rows * keys * lanes,
            transcendentals=2 * rows * keys,
            bytes_accessed=rows * lanes * 16 + CAP * shards * TILE * lanes * 4,
        ),
        name="random_attention",
    )(index, count, *flat, *whole, q, m, l, a)


def request_tables(random_tiles, random_count, shard, ctx_count, tiles_here):
    slots = random_tiles.shape[1]
    live = jnp.arange(slots, dtype=jnp.int32)[None, :] < random_count[:, None]
    entries = jnp.where(live, random_tiles, -1).reshape(ctx_count, tiles_here * slots)
    mine = shard * tiles_here + jnp.arange(tiles_here, dtype=jnp.int32)
    owned = jnp.any(entries[:, :, None] == mine[None, None, :], axis=1)
    k = jnp.arange(tiles_here, dtype=jnp.int32)
    rank = jnp.sum((owned[:, None, :] & (k[None, None, :] < k[None, :, None])).astype(jnp.int32), axis=2)
    hit = owned[:, None, :] & (rank[:, None, :] == jnp.arange(CAP, dtype=jnp.int32)[None, :, None])
    send = jnp.sum(jnp.where(hit, k[None, None, :], 0), axis=2)
    wanted = lax.dynamic_index_in_dim(entries, shard, 0, keepdims=False)
    tiles = jnp.arange(ctx_count * tiles_here, dtype=jnp.int32)
    needed = jnp.any(wanted[:, None] == tiles[None, :], axis=0)
    owner = wanted // tiles_here
    lower = (
        needed[None, :]
        & (tiles[None, :] < wanted[:, None])
        & (tiles[None, :] >= (owner * tiles_here)[:, None])
    )
    slot = jnp.sum(lower.astype(jnp.int32), axis=1)
    read = (slot * ctx_count + owner).reshape(tiles_here, slots)
    read = jnp.where(wanted.reshape(tiles_here, slots) >= 0, read, read[:, :1])
    return [send[:, slot] for slot in range(CAP)], read.reshape(-1)


def body(tokens, w_query, w_key, w_value, w_out, random_tiles, random_count):
    groups = lax.axis_size("head")
    ctx_count = lax.axis_size("ctx")
    rows, width = tokens.shape
    own_tiles = rows // TILE
    part = TILE // groups
    tiles_here = own_tiles * groups
    shard = lax.axis_index("ctx").astype(jnp.int32)

    here = lax.axis_index("head").astype(jnp.int32)

    striped = tokens.reshape(own_tiles, groups, part, width).transpose(1, 0, 2, 3)
    striped = lax.all_to_all(striped, "head", split_axis=0, concat_axis=0, tiled=True)
    striped = striped.reshape(tiles_here, part, width)
    send, read = request_tables(random_tiles, random_count, shard, ctx_count, tiles_here)
    head = here[None]

    own = project(head, [tokens], rows, [w_query, w_key, w_value], groups, place_rows)
    own = exchange(own, "head")

    up = [(i, i + 1) for i in range(ctx_count - 1)]
    down = [(j, i) for i, j in up]
    before = lax.ppermute(striped[-1:], "ctx", up)
    after = lax.ppermute(striped[:1], "ctx", down)
    edges = jnp.concatenate([before, after], axis=0).reshape(2 * part, width)

    fetched, got = [], None
    for slot in range(CAP - 1):
        chunks = pick_chunks(send[slot], striped, ctx_count, got)
        got = lax.all_to_all(chunks, "ctx", split_axis=0, concat_axis=0, tiled=True)
        count = ctx_count * part
        if slot == 0:
            xs, place, extra = [got], place_chunks, 0
        else:
            xs, place, extra = [got, edges], place_chunks_and_edges, (2 + GLOBALS) * part
        projected = project(head, xs, count, [w_key, w_value], groups, place, extra)
        if extra:
            ends = exchange(projected[groups:], "head")
        fetched.append(exchange(projected[:groups], "head"))
    chosen = pick_kv(send[CAP - 1], head, own, ctx_count)
    whole = lax.all_to_all(chosen, "ctx", split_axis=0, concat_axis=0, tiled=True)

    where = jnp.stack([shard, jnp.int32(tiles_here * ctx_count), here])
    m, l, a, q = local_attention(where, own, ends)
    my_count = lax.dynamic_slice_in_dim(random_count, shard * tiles_here, tiles_here, 0)
    attended = random_attention(read, my_count, q, fetched, [whole], m, l, a)
    attended = attended.reshape(groups, rows, -1)
    returned = lax.all_to_all(attended, "head", split_axis=0, concat_axis=0, tiled=True)
    out = lax.dot_general(
        returned,
        w_out.reshape(groups, -1, width),
        (((0, 2), (0, 1)), ((), ())),
        preferred_element_type=jnp.float32,
    )
    return out.astype(jnp.bfloat16)


def solution(mesh):
    return jax.shard_map(
        body,
        mesh=mesh,
        in_specs=(P(("ctx", "head"), None), P(), P(), P(), P(), P(), P()),
        out_specs=P(("ctx", "head"), None),
        check_vma=False,
    )
```

```python
import functools

import jax
import jax.numpy as jnp
from jax import lax
from jax.experimental import pallas as pl
from jax.experimental.pallas import tpu as pltpu
from jax.sharding import PartitionSpec as P


HEAD_DIM = 64
TILE = 128
GLOBALS = 2
RANDOM = 12
CAP = 3
LOG2E = 1.4426950408889634
SCALE = HEAD_DIM ** (-0.5) * LOG2E
NEG = -1e30
LANES = 128
SUB = 8


def project_kernel(here_ref, *refs, sources, weights, groups, place):
    x_refs, rest = refs[:sources], refs[sources:]
    w_refs, o_refs, x_ref = rest[:weights], rest[weights : weights + groups], rest[-1]
    e_refs = rest[weights + groups : -1]
    step = pl.program_id(0)

    @pl.when(step == 0)
    def _():
        place(x_ref, *x_refs)

    w = jnp.concatenate([ref[...] for ref in w_refs], axis=1)
    r = jnp.dot(x_ref[...], w, preferred_element_type=jnp.float32).astype(jnp.bfloat16)
    for o, o_ref in enumerate(o_refs):

        @pl.when(step == o)
        def _():
            o_ref[...] = r[: o_ref.shape[0]]
            if e_refs:
                e_refs[o][...] = r[o_ref.shape[0] :]


def place_rows(x_ref, rows_ref):
    x_ref[...] = rows_ref[...]


def place_chunks(x_ref, got_ref):
    shards, _, lanes = got_ref.shape
    part = x_ref.shape[0] // shards
    for k in range(x_ref.shape[1] // lanes):
        x_ref[:, k * lanes : (k + 1) * lanes] = got_ref[:, k * part : (k + 1) * part, :].reshape(
            shards * part, lanes
        )


def place_chunks_and_edges(x_ref, got_ref, edge_ref):
    shards, tall, lanes = got_ref.shape
    edges = edge_ref.shape[0]
    width = x_ref.shape[1]
    across = width // lanes
    extra = shards * SUB // across
    rows = x_ref.shape[0] - edges - extra
    place_chunks(x_ref.at[:rows], got_ref)
    x_ref[rows : rows + edges] = edge_ref[...]
    for b in range(shards):
        row = rows + edges + b // across * SUB
        lane = b % across * lanes
        x_ref[row : row + SUB, lane : lane + lanes] = got_ref[b, tall - SUB :, :]


def project(here, xs, rows, ws, groups, place, extra=0):
    width = ws[0].shape[0]
    lanes = ws[0].shape[1] // groups
    out_lanes = lanes * len(ws)
    outs = [(rows, out_lanes)] * groups + [(extra, out_lanes)] * (groups if extra else 0)
    rows = rows + extra
    return pl.pallas_call(
        functools.partial(
            project_kernel, sources=len(xs), weights=len(ws), groups=groups, place=place
        ),
        grid_spec=pltpu.PrefetchScalarGridSpec(
            num_scalar_prefetch=1,
            grid=(groups,),
            in_specs=[
                pl.BlockSpec(x.shape, lambda o, here, n=len(x.shape): (0,) * n) for x in xs
            ]
            + [
                pl.BlockSpec((width, lanes), lambda o, here: (0, lax.rem(here[0] + o, groups)))
                for _ in ws
            ],
            out_specs=[pl.BlockSpec(out, lambda o, here: (0, 0)) for out in outs],
            scratch_shapes=[pltpu.VMEM((rows, width), jnp.bfloat16)],
        ),
        out_shape=[jax.ShapeDtypeStruct(out, jnp.bfloat16) for out in outs],
        cost_estimate=pl.CostEstimate(
            flops=2 * rows * width * lanes * len(ws) * groups,
            transcendentals=0,
            bytes_accessed=2 * width * lanes * len(ws) * groups + 2 * rows * (width + out_lanes * groups),
        ),
    )(here, *xs, *ws)


def exchange(pieces, axis):
    size = len(pieces)
    return [pieces[0]] + [
        lax.ppermute(pieces[o], axis, [(i, (i + o) % size) for i in range(size)])
        for o in range(1, size)
    ]


def pick_chunk(o_ref, d, tile):
    lanes = o_ref.shape[2]
    part, width = tile.shape
    for k in range(width // lanes):
        o_ref[d, k * part : (k + 1) * part, :] = tile[:, k * lanes : (k + 1) * lanes]


def pick_kernel(index_ref, x_ref, o_ref, *, scatter):
    dests, tall, lanes = o_ref.shape
    part, width = x_ref.shape[1:]
    across = width // lanes

    def step(d, carry):
        pick_chunk(o_ref, d, x_ref[index_ref[d]])
        return carry

    lax.fori_loop(0, dests, step, 0)
    if scatter:
        for b in range(dests):
            row = b // across * SUB
            lane = b % across * lanes
            o_ref[b, tall - SUB :, :] = x_ref[
                row // part, row % part : row % part + SUB, lane : lane + lanes
            ]


def pick_chunks(index, x, dests, scatter):
    _, part, width = x.shape
    out = (dests, part * width // LANES + SUB, LANES)
    whole = lambda shape: pl.BlockSpec(shape, lambda i, idx: (0,) * len(shape))
    return pl.pallas_call(
        functools.partial(pick_kernel, scatter=scatter),
        grid_spec=pltpu.PrefetchScalarGridSpec(
            num_scalar_prefetch=1, grid=(1,), in_specs=[whole(x.shape)], out_specs=whole(out)
        ),
        out_shape=jax.ShapeDtypeStruct(out, x.dtype),
        cost_estimate=pl.CostEstimate(flops=0, transcendentals=0, bytes_accessed=4 * x.size * 2),
    )(index, x)


def insert_kernel(got_ref, chunks_ref, o_ref, block_ref, sem):
    _, sub, _ = block_ref.shape
    tall = o_ref.shape[1]
    block_ref[...] = jnp.broadcast_to(got_ref[...], block_ref.shape)
    copy = pltpu.make_async_copy(block_ref, o_ref.at[:, tall - sub :, :], sem)
    copy.start()
    copy.wait()


def insert_block(got, chunks):
    dests, tall, lanes = chunks.shape
    return pl.pallas_call(
        insert_kernel,
        grid=(1,),
        in_specs=[
            pl.BlockSpec((1, SUB, lanes), lambda i: (0, tall // SUB - 1, 0)),
            pl.BlockSpec(memory_space=pl.ANY),
        ],
        out_specs=pl.BlockSpec(memory_space=pl.ANY),
        out_shape=jax.ShapeDtypeStruct(chunks.shape, chunks.dtype),
        scratch_shapes=[pltpu.VMEM((dests, SUB, lanes), chunks.dtype), pltpu.SemaphoreType.DMA],
        input_output_aliases={1: 0},
        cost_estimate=pl.CostEstimate(
            flops=0, transcendentals=0, bytes_accessed=4 * dests * SUB * lanes
        ),
        name="insert_block",
    )(got, chunks)


def pick_kv_kernel(index_ref, here_ref, *refs):
    own_refs, (o_ref, kv_ref) = refs[:-2], refs[-2:]
    groups = len(own_refs)
    tiles = own_refs[0].shape[0] // TILE
    both = kv_ref.shape[2]
    lanes = own_refs[0].shape[1] - both
    for o, ref in enumerate(own_refs):
        home = lax.rem(here_ref[0] + groups - o, groups) * tiles
        for i in range(tiles):
            kv_ref[home + i] = ref[i * TILE : (i + 1) * TILE, lanes:]

    def step(d, carry):
        o_ref[d] = kv_ref[index_ref[d]]
        return carry

    lax.fori_loop(0, o_ref.shape[0], step, 0)


def pick_kv(index, here, own, dests):
    rows, lanes = own[0].shape
    both = lanes * 2 // 3
    out = (dests, TILE, both)
    return pl.pallas_call(
        pick_kv_kernel,
        grid_spec=pltpu.PrefetchScalarGridSpec(
            num_scalar_prefetch=2,
            grid=(1,),
            in_specs=[pl.BlockSpec((rows, lanes), lambda i, idx, here: (0, 0))] * len(own),
            out_specs=pl.BlockSpec(out, lambda i, idx, here: (0, 0, 0)),
            scratch_shapes=[pltpu.VMEM((len(own) * rows // TILE, TILE, both), jnp.bfloat16)],
        ),
        out_shape=jax.ShapeDtypeStruct(out, jnp.bfloat16),
        cost_estimate=pl.CostEstimate(
            flops=0, transcendentals=0, bytes_accessed=10 * len(own) * rows * lanes // 3
        ),
        name="pick_kv",
    )(index, here, *own)


def split_heads(q):
    first = lax.broadcasted_iota(jnp.int32, q.shape, 1) < HEAD_DIM
    zero = jnp.zeros_like(q)
    return jnp.concatenate([jnp.where(first, q, zero), jnp.where(first, zero, q)], axis=0)


def join_heads(both):
    half = both.shape[0] // 2
    shape = (half, 2 * HEAD_DIM)
    first = lax.broadcasted_iota(jnp.int32, shape, 1) < HEAD_DIM
    return jnp.where(
        first, jnp.broadcast_to(both[:half], shape), jnp.broadcast_to(both[half:], shape)
    )


def score(q2, keys):
    return lax.dot_general(q2, keys, (((1,), (1,)), ((), ())), preferred_element_type=jnp.float32)


def local_kernel(place_ref, *refs, groups):
    own_refs, ext_refs = refs[:groups], refs[groups : 2 * groups]
    m_ref, l_ref, a_ref, qo_ref, q_ref, pad_ref = refs[2 * groups :]
    own_rows = own_refs[0].shape[0]
    part = ext_refs[0].shape[0] // (2 + GLOBALS)
    tiles_here = own_rows * groups // TILE
    lanes = m_ref.shape[1]
    step = pl.program_id(0)
    per_step = m_ref.shape[0] // TILE

    @pl.when(step == 0)
    def _():
        homes = [0] + [tiles_here + 1 + i for i in range(1 + GLOBALS)]
        for o in range(groups):
            row = pl.multiple_of(lax.rem(place_ref[2] + groups - o, groups) * own_rows, own_rows)
            q_ref[pl.ds(row, own_rows), :] = own_refs[o][:, :lanes]
            pad_ref[pl.ds(row + TILE, own_rows), :] = own_refs[o][:, lanes:]
            for i, home in enumerate(homes):
                row = home * TILE + o * part
                pad_ref[row : row + part, :] = ext_refs[o][i * part : (i + 1) * part, :]

    tiles_total = place_ref[1]
    global_kv = pad_ref[(tiles_here + 2) * TILE :, :]
    ones = jnp.ones((3 * TILE, lanes), jnp.bfloat16)
    for i in range(per_step):
        t = step * per_step + i
        rows = pl.ds(i * TILE, TILE)
        q = q_ref[pl.ds(pl.multiple_of(t * TILE, TILE), TILE), :]
        q2 = split_heads(q)
        window = pad_ref[pl.ds(pl.multiple_of(t * TILE, TILE), 3 * TILE), :]
        first_id = place_ref[0] * tiles_here + t - 1
        position = lax.broadcasted_iota(jnp.int32, (2 * TILE, 3 * TILE), 1)
        ok = (position >= (GLOBALS - first_id) * TILE) & (
            position < (tiles_total - first_id) * TILE
        )
        s_window = jnp.where(ok, score(q2, window[:, :lanes]), NEG)
        s_global = score(q2, global_kv[:, :lanes])
        top = jnp.maximum(
            jnp.max(s_window, axis=1, keepdims=True), jnp.max(s_global, axis=1, keepdims=True)
        )
        p_window = jnp.exp2((s_window - top) * SCALE)
        p_global = jnp.exp2((s_global - top) * SCALE)
        acc = jnp.dot(
            p_window.astype(jnp.bfloat16),
            jnp.concatenate([window[:, lanes:], ones[: 3 * TILE]], axis=1),
            preferred_element_type=jnp.float32,
        ) + jnp.dot(
            p_global.astype(jnp.bfloat16),
            jnp.concatenate([global_kv[:, lanes:], ones[: GLOBALS * TILE]], axis=1),
            preferred_element_type=jnp.float32,
        )
        m_ref[rows, :] = join_heads(top)
        l_ref[rows, :] = join_heads(acc[:, lanes:])
        a_ref[rows, :] = join_heads(acc[:, :lanes])
        qo_ref[rows, :] = q


def local_attention(place, own, ext, per_step=4):
    groups = len(own)
    rows = own[0].shape[0] * groups
    both = ext[0].shape[1]
    lanes = both // 2
    block = pl.BlockSpec((per_step * TILE, lanes), lambda i, s: (i, 0))
    out = jax.ShapeDtypeStruct((rows, lanes), jnp.float32)
    keys = (3 + GLOBALS) * TILE
    return pl.pallas_call(
        functools.partial(local_kernel, groups=groups),
        grid_spec=pltpu.PrefetchScalarGridSpec(
            num_scalar_prefetch=1,
            grid=(rows // (per_step * TILE),),
            in_specs=[pl.BlockSpec(a.shape, lambda i, s: (0, 0)) for a in own]
            + [pl.BlockSpec(a.shape, lambda i, s: (0, 0)) for a in ext],
            out_specs=[block] * 4,
            scratch_shapes=[
                pltpu.VMEM((rows, lanes), jnp.bfloat16),
                pltpu.VMEM((rows + (2 + GLOBALS) * TILE, both), jnp.bfloat16),
            ],
        ),
        out_shape=[out] * 3 + [jax.ShapeDtypeStruct((rows, lanes), jnp.bfloat16)],
        cost_estimate=pl.CostEstimate(
            flops=8 * rows * keys * lanes,
            transcendentals=2 * rows * keys,
            bytes_accessed=rows * lanes * 20,
        ),
        name="local_attention",
    )(place, *own, *ext)


def random_kernel(index_ref, count_ref, *refs, groups, spread, half):
    part_refs, whole_refs = refs[: spread * groups], refs[spread * groups : spread * groups + CAP - spread]
    q_ref, m_ref, l_ref, a_ref, o_ref, kv_ref, sems = refs[spread * groups + CAP - spread :]
    pieces, _, piece, lanes = q_ref.shape
    halves = index_ref.shape[0] // (RANDOM * groups * (piece // TILE))
    step = pl.program_id(0)
    part = TILE // groups
    shards = kv_ref.shape[0] // CAP

    @pl.when(step == 0)
    def _():
        copies = []
        for i, ref in enumerate(part_refs):
            s, o = divmod(i, groups)
            home = kv_ref.at[s * shards : (s + 1) * shards, o * part : (o + 1) * part, :]
            copies.append(pltpu.make_async_copy(ref.at[:shards], home, sems.at[i]))
        for i, ref in enumerate(whole_refs):
            home = kv_ref.at[(spread + i) * shards : (spread + i + 1) * shards]
            copies.append(pltpu.make_async_copy(ref, home, sems.at[spread * groups + i]))
        for copy in copies:
            copy.start()
        for copy in copies:
            copy.wait()

    for i in range(pieces * piece // TILE):
        home, sub = divmod(i, piece // TILE)
        t = ((step * pieces + home) * halves + half) * (piece // TILE) + sub
        rows = (home, 0, pl.ds(sub * TILE, TILE))
        q2 = split_heads(q_ref[rows])
        count = count_ref[t]
        at = [index_ref[t * RANDOM + j] for j in range(RANDOM)]
        scores = []
        top = None
        for j in range(0, RANDOM, 2):
            keys = jnp.concatenate([kv_ref[at[j], :, :lanes], kv_ref[at[j + 1], :, :lanes]], axis=0)
            s = score(q2, keys)
            scores.append(s)
            top = s if top is None else jnp.maximum(top, s)
        m_old = m_ref[rows]
        m_old = jnp.concatenate([m_old[:, :1], m_old[:, HEAD_DIM : HEAD_DIM + 1]], axis=0)
        m_new = jnp.maximum(jnp.max(top, axis=1, keepdims=True), m_old)
        alpha = jnp.exp2((m_old - m_new) * SCALE)
        acc = None
        for j in range(0, RANDOM, 2):
            p = jnp.exp2((scores[j // 2] - m_new) * SCALE).astype(jnp.bfloat16)
            v = []
            for i in range(j, j + 2):
                live = jnp.where(i < count, 1.0, 0.0).astype(jnp.float32)
                one = jnp.full((TILE, lanes), live, jnp.float32).astype(jnp.bfloat16)
                v.append(jnp.concatenate([kv_ref[at[i], :, lanes:] * one, one], axis=1))
            part = jnp.dot(p, jnp.concatenate(v, axis=0), preferred_element_type=jnp.float32)
            acc = part if acc is None else acc + part
        total = acc[:, lanes:]
        acc = acc[:, :lanes]
        alpha = join_heads(alpha)
        denominator = l_ref[rows] * alpha + join_heads(total)
        numerator = a_ref[rows] * alpha + join_heads(acc)
        o_ref[home, pl.ds(sub * TILE, TILE)] = (numerator / denominator).astype(jnp.bfloat16)


def random_attention(index, count, q, parts, whole, m, l, a, half, halves, pieces=4):
    rows, lanes = q.shape
    groups = len(parts[0])
    spread = len(parts)
    shards = whole[0].shape[0]
    part = TILE // groups
    flat = [f.reshape(-1, part, 2 * lanes) for slot in parts for f in slot]
    piece = rows // (groups * halves)
    block = pl.BlockSpec((pieces, 1, piece, lanes), lambda i, s, c: (i, half, 0, 0))
    views = [x.reshape(groups, halves, piece, lanes) for x in (q, m, l, a)]
    keys = RANDOM * TILE
    sources = len(flat) + len(whole)
    return pl.pallas_call(
        functools.partial(random_kernel, groups=groups, spread=spread, half=half),
        grid_spec=pltpu.PrefetchScalarGridSpec(
            num_scalar_prefetch=2,
            grid=(groups // pieces,),
            in_specs=[pl.BlockSpec(memory_space=pl.ANY)] * sources + [block] * 4,
            out_specs=pl.BlockSpec((pieces, piece, lanes), lambda i, s, c: (i, 0, 0)),
            scratch_shapes=[
                pltpu.VMEM((CAP * shards, TILE, 2 * lanes), jnp.bfloat16),
                pltpu.SemaphoreType.DMA((sources,)),
            ],
        ),
        out_shape=jax.ShapeDtypeStruct((groups, piece, lanes), jnp.bfloat16),
        cost_estimate=pl.CostEstimate(
            flops=8 * rows * keys * lanes // halves,
            transcendentals=2 * rows * keys // halves,
            bytes_accessed=rows * lanes * 16 + CAP * shards * TILE * lanes * 4,
        ),
    )(index, count, *flat, *whole, *views)


def request_tables(random_tiles, random_count, shard, ctx_count, tiles_here):
    slots = random_tiles.shape[1]
    live = jnp.arange(slots, dtype=jnp.int32)[None, :] < random_count[:, None]
    entries = jnp.where(live, random_tiles, -1).reshape(ctx_count, tiles_here * slots)
    mine = shard * tiles_here + jnp.arange(tiles_here, dtype=jnp.int32)
    owned = jnp.any(entries[:, :, None] == mine[None, None, :], axis=1)
    k = jnp.arange(tiles_here, dtype=jnp.int32)
    rank = jnp.sum((owned[:, None, :] & (k[None, None, :] < k[None, :, None])).astype(jnp.int32), axis=2)
    hit = owned[:, None, :] & (rank[:, None, :] == jnp.arange(CAP, dtype=jnp.int32)[None, :, None])
    send = jnp.sum(jnp.where(hit, k[None, None, :], 0), axis=2)
    wanted = lax.dynamic_index_in_dim(entries, shard, 0, keepdims=False)
    tiles = jnp.arange(ctx_count * tiles_here, dtype=jnp.int32)
    needed = jnp.any(wanted[:, None] == tiles[None, :], axis=0)
    owner = wanted // tiles_here
    lower = (
        needed[None, :]
        & (tiles[None, :] < wanted[:, None])
        & (tiles[None, :] >= (owner * tiles_here)[:, None])
    )
    slot = jnp.sum(lower.astype(jnp.int32), axis=1)
    read = (slot * ctx_count + owner).reshape(tiles_here, slots)
    read = jnp.where(wanted.reshape(tiles_here, slots) >= 0, read, read[:, :1])
    return [send[:, slot] for slot in range(CAP)], read.reshape(-1)


def body(tokens, w_query, w_key, w_value, w_out, random_tiles, random_count):
    groups = lax.axis_size("head")
    ctx_count = lax.axis_size("ctx")
    rows, width = tokens.shape
    own_tiles = rows // TILE
    part = TILE // groups
    tiles_here = own_tiles * groups
    shard = lax.axis_index("ctx").astype(jnp.int32)

    here = lax.axis_index("head").astype(jnp.int32)

    striped = tokens.reshape(own_tiles, groups, part, width).transpose(1, 0, 2, 3)
    striped = lax.all_to_all(striped, "head", split_axis=0, concat_axis=0, tiled=True)
    striped = striped.reshape(tiles_here, part, width)
    send, read = request_tables(random_tiles, random_count, shard, ctx_count, tiles_here)
    head = here[None]

    own = project(head, [tokens], rows, [w_query, w_key, w_value], groups, place_rows)
    own = exchange(own, "head")

    up = [(i, i + 1) for i in range(ctx_count - 1)]
    down = [(j, i) for i, j in up]
    before = lax.ppermute(striped[-1:], "ctx", up)
    after = lax.ppermute(striped[:1], "ctx", down)
    edges = jnp.concatenate([before, after], axis=0).reshape(2 * part, width)

    fetched, got = [], None
    for slot in range(CAP - 1):
        chunks = pick_chunks(send[slot], striped, ctx_count, slot == 0)
        if slot:
            chunks = insert_block(got, chunks)
        got = lax.all_to_all(chunks, "ctx", split_axis=0, concat_axis=0, tiled=True)
        count = ctx_count * part
        if slot == 0:
            xs, place, extra = [got], place_chunks, 0
        else:
            xs, place, extra = [got, edges], place_chunks_and_edges, (2 + GLOBALS) * part
        projected = project(head, xs, count, [w_key, w_value], groups, place, extra)
        if extra:
            ends = exchange(projected[groups:], "head")
        fetched.append(exchange(projected[:groups], "head"))
    chosen = pick_kv(send[CAP - 1], head, own, ctx_count)
    whole = lax.all_to_all(chosen, "ctx", split_axis=0, concat_axis=0, tiled=True)

    where = jnp.stack([shard, jnp.int32(tiles_here * ctx_count), here])
    m, l, a, q = local_attention(where, own, ends)
    my_count = lax.dynamic_slice_in_dim(random_count, shard * tiles_here, tiles_here, 0)
    outs = []
    for half in range(2):
        mixed = random_attention(
            read, my_count, q, fetched, [whole], m, l, a, half, 2, 4 - 2 * half
        )
        back = lax.all_to_all(mixed, "head", split_axis=0, concat_axis=0, tiled=True)
        out = lax.dot_general(
            back,
            w_out.reshape(groups, -1, width),
            (((0, 2), (0, 1)), ((), ())),
            preferred_element_type=jnp.float32,
        )
        outs.append(out.astype(jnp.bfloat16))
    return jnp.concatenate(outs, axis=0)


def solution(mesh):
    return jax.shard_map(
        body,
        mesh=mesh,
        in_specs=(P(("ctx", "head"), None), P(), P(), P(), P(), P(), P()),
        out_specs=P(("ctx", "head"), None),
        check_vma=False,
    )
```

```python
import functools

import jax
import jax.numpy as jnp
from jax import lax
from jax.experimental import pallas as pl
from jax.experimental.pallas import tpu as pltpu
from jax.sharding import PartitionSpec as P


HEAD_DIM = 64
TILE = 128
GLOBALS = 2
RANDOM = 12
CAP = 3
LOG2E = 1.4426950408889634
SCALE = HEAD_DIM ** (-0.5) * LOG2E
NEG = -1e30
LANES = 128
SUB = 8


def project_kernel(here_ref, *refs, sources, weights, groups, place):
    x_refs, rest = refs[:sources], refs[sources:]
    w_refs, o_refs, x_ref = rest[:weights], rest[weights : weights + groups], rest[-1]
    e_refs = rest[weights + groups : -1]
    step = pl.program_id(0)

    @pl.when(step == 0)
    def _():
        place(x_ref, *x_refs)

    w = jnp.concatenate([ref[...] for ref in w_refs], axis=1)
    r = jnp.dot(x_ref[...], w, preferred_element_type=jnp.float32).astype(jnp.bfloat16)
    for o, o_ref in enumerate(o_refs):

        @pl.when(step == o)
        def _():
            o_ref[...] = r[: o_ref.shape[0]]
            if e_refs:
                e_refs[o][...] = r[o_ref.shape[0] :]


def place_rows(x_ref, rows_ref):
    x_ref[...] = rows_ref[...]


def place_chunks(x_ref, got_ref):
    shards, _, lanes = got_ref.shape
    part = x_ref.shape[0] // shards
    for k in range(x_ref.shape[1] // lanes):
        x_ref[:, k * lanes : (k + 1) * lanes] = got_ref[:, k * part : (k + 1) * part, :].reshape(
            shards * part, lanes
        )


def place_chunks_and_edges(x_ref, got_ref, edge_ref):
    shards, tall, lanes = got_ref.shape
    edges = edge_ref.shape[0]
    width = x_ref.shape[1]
    across = width // lanes
    extra = shards * SUB // across
    rows = x_ref.shape[0] - edges - extra
    place_chunks(x_ref.at[:rows], got_ref)
    x_ref[rows : rows + edges] = edge_ref[...]
    for b in range(shards):
        row = rows + edges + b // across * SUB
        lane = b % across * lanes
        x_ref[row : row + SUB, lane : lane + lanes] = got_ref[b, tall - SUB :, :]


def project(here, xs, rows, ws, groups, place, extra=0):
    width = ws[0].shape[0]
    lanes = ws[0].shape[1] // groups
    out_lanes = lanes * len(ws)
    outs = [(rows, out_lanes)] * groups + [(extra, out_lanes)] * (groups if extra else 0)
    rows = rows + extra
    return pl.pallas_call(
        functools.partial(
            project_kernel, sources=len(xs), weights=len(ws), groups=groups, place=place
        ),
        grid_spec=pltpu.PrefetchScalarGridSpec(
            num_scalar_prefetch=1,
            grid=(groups,),
            in_specs=[
                pl.BlockSpec(x.shape, lambda o, here, n=len(x.shape): (0,) * n) for x in xs
            ]
            + [
                pl.BlockSpec((width, lanes), lambda o, here: (0, lax.rem(here[0] + o, groups)))
                for _ in ws
            ],
            out_specs=[pl.BlockSpec(out, lambda o, here: (0, 0)) for out in outs],
            scratch_shapes=[pltpu.VMEM((rows, width), jnp.bfloat16)],
        ),
        out_shape=[jax.ShapeDtypeStruct(out, jnp.bfloat16) for out in outs],
        cost_estimate=pl.CostEstimate(
            flops=2 * rows * width * lanes * len(ws) * groups,
            transcendentals=0,
            bytes_accessed=2 * width * lanes * len(ws) * groups + 2 * rows * (width + out_lanes * groups),
        ),
    )(here, *xs, *ws)


def exchange(pieces, axis):
    size = len(pieces)
    return [pieces[0]] + [
        lax.ppermute(pieces[o], axis, [(i, (i + o) % size) for i in range(size)])
        for o in range(1, size)
    ]


def pick_chunk(o_ref, d, tile):
    lanes = o_ref.shape[2]
    part, width = tile.shape
    for k in range(width // lanes):
        o_ref[d, k * part : (k + 1) * part, :] = tile[:, k * lanes : (k + 1) * lanes]


def pick_kernel(index_ref, x_ref, o_ref, *, scatter):
    dests, tall, lanes = o_ref.shape
    part, width = x_ref.shape[1:]
    across = width // lanes

    def step(d, carry):
        pick_chunk(o_ref, d, x_ref[index_ref[d]])
        return carry

    lax.fori_loop(0, dests, step, 0)
    if scatter:
        for b in range(dests):
            row = b // across * SUB
            lane = b % across * lanes
            o_ref[b, tall - SUB :, :] = x_ref[
                row // part, row % part : row % part + SUB, lane : lane + lanes
            ]


def pick_chunks(index, x, dests, scatter):
    _, part, width = x.shape
    out = (dests, part * width // LANES + SUB, LANES)
    whole = lambda shape: pl.BlockSpec(shape, lambda i, idx: (0,) * len(shape))
    return pl.pallas_call(
        functools.partial(pick_kernel, scatter=scatter),
        grid_spec=pltpu.PrefetchScalarGridSpec(
            num_scalar_prefetch=1, grid=(1,), in_specs=[whole(x.shape)], out_specs=whole(out)
        ),
        out_shape=jax.ShapeDtypeStruct(out, x.dtype),
        cost_estimate=pl.CostEstimate(flops=0, transcendentals=0, bytes_accessed=4 * x.size * 2),
    )(index, x)


def insert_kernel(got_ref, chunks_ref, o_ref, block_ref, sem):
    _, sub, _ = block_ref.shape
    tall = o_ref.shape[1]
    block_ref[...] = jnp.broadcast_to(got_ref[...], block_ref.shape)
    copy = pltpu.make_async_copy(block_ref, o_ref.at[:, tall - sub :, :], sem)
    copy.start()
    copy.wait()


def insert_block(got, chunks):
    dests, tall, lanes = chunks.shape
    return pl.pallas_call(
        insert_kernel,
        grid=(1,),
        in_specs=[
            pl.BlockSpec((1, SUB, lanes), lambda i: (0, tall // SUB - 1, 0)),
            pl.BlockSpec(memory_space=pl.ANY),
        ],
        out_specs=pl.BlockSpec(memory_space=pl.ANY),
        out_shape=jax.ShapeDtypeStruct(chunks.shape, chunks.dtype),
        scratch_shapes=[pltpu.VMEM((dests, SUB, lanes), chunks.dtype), pltpu.SemaphoreType.DMA],
        input_output_aliases={1: 0},
        cost_estimate=pl.CostEstimate(
            flops=0, transcendentals=0, bytes_accessed=4 * dests * SUB * lanes
        ),
        name="insert_block",
    )(got, chunks)


def pick_kv_kernel(index_ref, here_ref, *refs):
    own_refs, (o_ref, kv_ref) = refs[:-2], refs[-2:]
    groups = len(own_refs)
    tiles = own_refs[0].shape[0] // TILE
    both = kv_ref.shape[2]
    lanes = own_refs[0].shape[1] - both
    for o, ref in enumerate(own_refs):
        home = lax.rem(here_ref[0] + groups - o, groups) * tiles
        for i in range(tiles):
            kv_ref[home + i] = ref[i * TILE : (i + 1) * TILE, lanes:]

    def step(d, carry):
        o_ref[d] = kv_ref[index_ref[d]]
        return carry

    lax.fori_loop(0, o_ref.shape[0], step, 0)


def pick_kv(index, here, own, dests):
    rows, lanes = own[0].shape
    both = lanes * 2 // 3
    out = (dests, TILE, both)
    return pl.pallas_call(
        pick_kv_kernel,
        grid_spec=pltpu.PrefetchScalarGridSpec(
            num_scalar_prefetch=2,
            grid=(1,),
            in_specs=[pl.BlockSpec((rows, lanes), lambda i, idx, here: (0, 0))] * len(own),
            out_specs=pl.BlockSpec(out, lambda i, idx, here: (0, 0, 0)),
            scratch_shapes=[pltpu.VMEM((len(own) * rows // TILE, TILE, both), jnp.bfloat16)],
        ),
        out_shape=jax.ShapeDtypeStruct(out, jnp.bfloat16),
        cost_estimate=pl.CostEstimate(
            flops=0, transcendentals=0, bytes_accessed=10 * len(own) * rows * lanes // 3
        ),
        name="pick_kv",
    )(index, here, *own)


def split_heads(q):
    first = lax.broadcasted_iota(jnp.int32, q.shape, 1) < HEAD_DIM
    zero = jnp.zeros_like(q)
    return jnp.concatenate([jnp.where(first, q, zero), jnp.where(first, zero, q)], axis=0)


def join_heads(both):
    half = both.shape[0] // 2
    shape = (half, 2 * HEAD_DIM)
    first = lax.broadcasted_iota(jnp.int32, shape, 1) < HEAD_DIM
    return jnp.where(
        first, jnp.broadcast_to(both[:half], shape), jnp.broadcast_to(both[half:], shape)
    )


def score(q2, keys):
    return lax.dot_general(q2, keys, (((1,), (1,)), ((), ())), preferred_element_type=jnp.float32)


def local_kernel(place_ref, *refs, groups):
    own_refs, ext_refs = refs[:groups], refs[groups : 2 * groups]
    m_ref, l_ref, a_ref, qo_ref, q_ref, pad_ref = refs[2 * groups :]
    own_rows = own_refs[0].shape[0]
    part = ext_refs[0].shape[0] // (2 + GLOBALS)
    tiles_here = own_rows * groups // TILE
    lanes = m_ref.shape[1]
    step = pl.program_id(0)
    per_step = m_ref.shape[0] // TILE

    @pl.when(step == 0)
    def _():
        homes = [0] + [tiles_here + 1 + i for i in range(1 + GLOBALS)]
        for o in range(groups):
            row = pl.multiple_of(lax.rem(place_ref[2] + groups - o, groups) * own_rows, own_rows)
            q_ref[pl.ds(row, own_rows), :] = own_refs[o][:, :lanes]
            pad_ref[pl.ds(row + TILE, own_rows), :] = own_refs[o][:, lanes:]
            for i, home in enumerate(homes):
                row = home * TILE + o * part
                pad_ref[row : row + part, :] = ext_refs[o][i * part : (i + 1) * part, :]

    tiles_total = place_ref[1]
    global_kv = pad_ref[(tiles_here + 2) * TILE :, :]
    ones = jnp.ones((3 * TILE, lanes), jnp.bfloat16)
    for i in range(per_step):
        t = step * per_step + i
        rows = pl.ds(i * TILE, TILE)
        q = q_ref[pl.ds(pl.multiple_of(t * TILE, TILE), TILE), :]
        q2 = split_heads(q)
        window = pad_ref[pl.ds(pl.multiple_of(t * TILE, TILE), 3 * TILE), :]
        first_id = place_ref[0] * tiles_here + t - 1
        position = lax.broadcasted_iota(jnp.int32, (2 * TILE, 3 * TILE), 1)
        ok = (position >= (GLOBALS - first_id) * TILE) & (
            position < (tiles_total - first_id) * TILE
        )
        s_window = jnp.where(ok, score(q2, window[:, :lanes]), NEG)
        s_global = score(q2, global_kv[:, :lanes])
        top = jnp.maximum(
            jnp.max(s_window, axis=1, keepdims=True), jnp.max(s_global, axis=1, keepdims=True)
        )
        p_window = jnp.exp2((s_window - top) * SCALE)
        p_global = jnp.exp2((s_global - top) * SCALE)
        acc = jnp.dot(
            p_window.astype(jnp.bfloat16),
            jnp.concatenate([window[:, lanes:], ones[: 3 * TILE]], axis=1),
            preferred_element_type=jnp.float32,
        ) + jnp.dot(
            p_global.astype(jnp.bfloat16),
            jnp.concatenate([global_kv[:, lanes:], ones[: GLOBALS * TILE]], axis=1),
            preferred_element_type=jnp.float32,
        )
        m_ref[rows, :] = join_heads(top)
        l_ref[rows, :] = join_heads(acc[:, lanes:])
        a_ref[rows, :] = join_heads(acc[:, :lanes])
        qo_ref[rows, :] = q


def local_attention(place, own, ext, per_step=4):
    groups = len(own)
    rows = own[0].shape[0] * groups
    both = ext[0].shape[1]
    lanes = both // 2
    block = pl.BlockSpec((per_step * TILE, lanes), lambda i, s: (i, 0))
    out = jax.ShapeDtypeStruct((rows, lanes), jnp.float32)
    keys = (3 + GLOBALS) * TILE
    return pl.pallas_call(
        functools.partial(local_kernel, groups=groups),
        grid_spec=pltpu.PrefetchScalarGridSpec(
            num_scalar_prefetch=1,
            grid=(rows // (per_step * TILE),),
            in_specs=[pl.BlockSpec(a.shape, lambda i, s: (0, 0)) for a in own]
            + [pl.BlockSpec(a.shape, lambda i, s: (0, 0)) for a in ext],
            out_specs=[block] * 4,
            scratch_shapes=[
                pltpu.VMEM((rows, lanes), jnp.bfloat16),
                pltpu.VMEM((rows + (2 + GLOBALS) * TILE, both), jnp.bfloat16),
            ],
        ),
        out_shape=[out] * 3 + [jax.ShapeDtypeStruct((rows, lanes), jnp.bfloat16)],
        cost_estimate=pl.CostEstimate(
            flops=8 * rows * keys * lanes,
            transcendentals=2 * rows * keys,
            bytes_accessed=rows * lanes * 20,
        ),
        name="local_attention",
    )(place, *own, *ext)


def random_kernel(index_ref, count_ref, *refs, groups, spread):
    part_refs, whole_refs = refs[: spread * groups], refs[spread * groups : spread * groups + CAP - spread]
    q_ref, m_ref, l_ref, a_ref, o_ref, kv_ref, sems = refs[spread * groups + CAP - spread :]
    lanes = q_ref.shape[1]
    step = pl.program_id(0)
    per_step = q_ref.shape[0] // TILE
    part = TILE // groups
    shards = kv_ref.shape[0] // CAP

    @pl.when(step == 0)
    def _():
        copies = []
        for i, ref in enumerate(part_refs):
            s, o = divmod(i, groups)
            home = kv_ref.at[s * shards : (s + 1) * shards, o * part : (o + 1) * part, :]
            copies.append(pltpu.make_async_copy(ref.at[:shards], home, sems.at[i]))
        for i, ref in enumerate(whole_refs):
            home = kv_ref.at[(spread + i) * shards : (spread + i + 1) * shards]
            copies.append(pltpu.make_async_copy(ref, home, sems.at[spread * groups + i]))
        for copy in copies:
            copy.start()
        for copy in copies:
            copy.wait()

    for i in range(per_step):
        t = step * per_step + i
        rows = pl.ds(i * TILE, TILE)
        q2 = split_heads(q_ref[rows, :])
        count = count_ref[t]
        at = [index_ref[t * RANDOM + j] for j in range(RANDOM)]
        scores = []
        top = None
        for j in range(0, RANDOM, 2):
            keys = jnp.concatenate([kv_ref[at[j], :, :lanes], kv_ref[at[j + 1], :, :lanes]], axis=0)
            s = score(q2, keys)
            scores.append(s)
            top = s if top is None else jnp.maximum(top, s)
        m_old = m_ref[rows, :]
        m_old = jnp.concatenate([m_old[:, :1], m_old[:, HEAD_DIM : HEAD_DIM + 1]], axis=0)
        m_new = jnp.maximum(jnp.max(top, axis=1, keepdims=True), m_old)
        alpha = jnp.exp2((m_old - m_new) * SCALE)
        acc = None
        for j in range(0, RANDOM, 2):
            p = jnp.exp2((scores[j // 2] - m_new) * SCALE).astype(jnp.bfloat16)
            v = []
            for i in range(j, j + 2):
                live = jnp.where(i < count, 1.0, 0.0).astype(jnp.float32)
                one = jnp.full((TILE, lanes), live, jnp.float32).astype(jnp.bfloat16)
                v.append(jnp.concatenate([kv_ref[at[i], :, lanes:] * one, one], axis=1))
            part = jnp.dot(p, jnp.concatenate(v, axis=0), preferred_element_type=jnp.float32)
            acc = part if acc is None else acc + part
        total = acc[:, lanes:]
        acc = acc[:, :lanes]
        alpha = join_heads(alpha)
        denominator = l_ref[rows, :] * alpha + join_heads(total)
        numerator = a_ref[rows, :] * alpha + join_heads(acc)
        o_ref[rows, :] = (numerator / denominator).astype(jnp.bfloat16)


def random_attention(index, count, q, parts, whole, m, l, a, per_step=8):
    rows, lanes = q.shape
    groups = len(parts[0])
    spread = len(parts)
    shards = whole[0].shape[0]
    part = TILE // groups
    flat = [f.reshape(-1, part, 2 * lanes) for slot in parts for f in slot]
    block = pl.BlockSpec((per_step * TILE, lanes), lambda i, s, c: (i, 0))
    keys = RANDOM * TILE
    sources = len(flat) + len(whole)
    return pl.pallas_call(
        functools.partial(random_kernel, groups=groups, spread=spread),
        grid_spec=pltpu.PrefetchScalarGridSpec(
            num_scalar_prefetch=2,
            grid=(rows // (per_step * TILE),),
            in_specs=[pl.BlockSpec(memory_space=pl.ANY)] * sources + [block] * 4,
            out_specs=block,
            scratch_shapes=[
                pltpu.VMEM((CAP * shards, TILE, 2 * lanes), jnp.bfloat16),
                pltpu.SemaphoreType.DMA((sources,)),
            ],
        ),
        out_shape=jax.ShapeDtypeStruct((rows, lanes), jnp.bfloat16),
        cost_estimate=pl.CostEstimate(
            flops=8 * rows * keys * lanes,
            transcendentals=2 * rows * keys,
            bytes_accessed=rows * lanes * 16 + CAP * shards * TILE * lanes * 4,
        ),
        name="random_attention",
    )(index, count, *flat, *whole, q, m, l, a)


def request_tables(random_tiles, random_count, shard, ctx_count, tiles_here):
    slots = random_tiles.shape[1]
    live = jnp.arange(slots, dtype=jnp.int32)[None, :] < random_count[:, None]
    entries = jnp.where(live, random_tiles, -1).reshape(ctx_count, tiles_here * slots)
    mine = shard * tiles_here + jnp.arange(tiles_here, dtype=jnp.int32)
    owned = jnp.any(entries[:, :, None] == mine[None, None, :], axis=1)
    k = jnp.arange(tiles_here, dtype=jnp.int32)
    rank = jnp.sum((owned[:, None, :] & (k[None, None, :] < k[None, :, None])).astype(jnp.int32), axis=2)
    hit = owned[:, None, :] & (rank[:, None, :] == jnp.arange(CAP, dtype=jnp.int32)[None, :, None])
    send = jnp.sum(jnp.where(hit, k[None, None, :], 0), axis=2)
    wanted = lax.dynamic_index_in_dim(entries, shard, 0, keepdims=False)
    tiles = jnp.arange(ctx_count * tiles_here, dtype=jnp.int32)
    needed = jnp.any(wanted[:, None] == tiles[None, :], axis=0)
    owner = wanted // tiles_here
    lower = (
        needed[None, :]
        & (tiles[None, :] < wanted[:, None])
        & (tiles[None, :] >= (owner * tiles_here)[:, None])
    )
    slot = jnp.sum(lower.astype(jnp.int32), axis=1)
    read = (slot * ctx_count + owner).reshape(tiles_here, slots)
    read = jnp.where(wanted.reshape(tiles_here, slots) >= 0, read, read[:, :1])
    return [send[:, slot] for slot in range(CAP)], read.reshape(-1)


def body(tokens, w_query, w_key, w_value, w_out, random_tiles, random_count):
    groups = lax.axis_size("head")
    ctx_count = lax.axis_size("ctx")
    rows, width = tokens.shape
    own_tiles = rows // TILE
    part = TILE // groups
    tiles_here = own_tiles * groups
    shard = lax.axis_index("ctx").astype(jnp.int32)

    here = lax.axis_index("head").astype(jnp.int32)

    striped = tokens.reshape(own_tiles, groups, part, width).transpose(1, 0, 2, 3)
    striped = lax.all_to_all(striped, "head", split_axis=0, concat_axis=0, tiled=True)
    striped = striped.reshape(tiles_here, part, width)
    send, read = request_tables(random_tiles, random_count, shard, ctx_count, tiles_here)
    head = here[None]

    own = project(head, [tokens], rows, [w_query, w_key, w_value], groups, place_rows)
    own = exchange(own, "head")

    up = [(i, i + 1) for i in range(ctx_count - 1)]
    down = [(j, i) for i, j in up]
    before = lax.ppermute(striped[-1:], "ctx", up)
    after = lax.ppermute(striped[:1], "ctx", down)
    edges = jnp.concatenate([before, after], axis=0).reshape(2 * part, width)

    fetched, got = [], None
    for slot in range(CAP - 1):
        chunks = pick_chunks(send[slot], striped, ctx_count, slot == 0)
        if slot:
            chunks = insert_block(got, chunks)
        got = lax.all_to_all(chunks, "ctx", split_axis=0, concat_axis=0, tiled=True)
        count = ctx_count * part
        if slot == 0:
            xs, place, extra = [got], place_chunks, 0
        else:
            xs, place, extra = [got, edges], place_chunks_and_edges, (2 + GLOBALS) * part
        projected = project(head, xs, count, [w_key, w_value], groups, place, extra)
        if extra:
            ends = exchange(projected[groups:], "head")
        fetched.append(exchange(projected[:groups], "head"))
    chosen = pick_kv(send[CAP - 1], head, own, ctx_count)
    whole = lax.all_to_all(chosen, "ctx", split_axis=0, concat_axis=0, tiled=True)

    where = jnp.stack([shard, jnp.int32(tiles_here * ctx_count), here])
    m, l, a, q = local_attention(where, own, ends)
    my_count = lax.dynamic_slice_in_dim(random_count, shard * tiles_here, tiles_here, 0)
    attended = random_attention(read, my_count, q, fetched, [whole], m, l, a)
    attended = attended.reshape(groups, rows, -1)
    returned = lax.all_to_all(attended, "head", split_axis=0, concat_axis=0, tiled=True)
    out = lax.dot_general(
        returned,
        w_out.reshape(groups, -1, width),
        (((0, 2), (0, 1)), ((), ())),
        preferred_element_type=jnp.float32,
    )
    return out.astype(jnp.bfloat16)


def solution(mesh):
    return jax.shard_map(
        body,
        mesh=mesh,
        in_specs=(P(("ctx", "head"), None), P(), P(), P(), P(), P(), P()),
        out_specs=P(("ctx", "head"), None),
        check_vma=False,
    )
```
